256 devices in a mesh: rep: 2 (over z_hi), kv: 32 (over y, x, core), tp: 4 (over z_lo).
Axes of the slice: x: 4, y: 4, z: 8 (z_hi: 2, z_lo: 4; z = z_hi * 4 + z_lo), core: 2. Of those that a mesh axis runs over, the one named last changes fastest.
Arguments:
- token_state: bfloat16 [256, 1280], P('kv'), may hold values from -6 to 6
- attn_gain: float32 [1280], replicated, may hold values from 0.1 to 1.9
- qkv_weight: bfloat16 [1280, 3840], P(None, 'tp'), may hold values from -0.15625 to 0.15625
- out_weight: bfloat16 [1280, 1280], P('tp'), may hold values from -0.15625 to 0.15625
- mlp_gain: float32 [1280], replicated, may hold values from 0.1 to 1.9
- up_weight: bfloat16 [1280, 1280], P(None, 'tp'), may hold values from -0.15625 to 0.15625
- down_weight: bfloat16 [1280, 1280], P('tp'), may hold values from -0.15625 to 0.15625
- kv_cache: bfloat16 [2, 352, 512, 2560], P('rep', 'kv', None, 'tp'), as said below
- home_replica: int32 [256], replicated, may hold values from 0 to 1, as said below
- moving: int32 [256], replicated, may hold values 0 or 1
- cache_length: int32 [256], replicated, may hold values from 1 to 32768, as said below
- block_owner: int32 [2, 352], P('rep', 'kv'), may hold values from 0 to 256, as said below
- block_index: int32 [2, 352], P('rep', 'kv'), may hold values from 0 to 63, as said below
Outputs:
- hidden_out: float32 [2, 256, 1280], P('rep', 'kv')
- new_entries: float32 [2, 256, 2560], P('rep', 'kv', 'tp')
The draws below stay inside these ranges and needn't reach their ends.
Inputs may be any that keep to these rules, and one draw needn't show every extreme that they name: `home_replica`: both replicas hold at least one slot. `cache_length`: a slot's cache lies whole in the pool of its home replica; one slot of each replica has exactly 32768 tokens. `block_owner`: a slot owns exactly ceil(cache_length / 512) blocks, all in the pool of its home replica; 256 marks a free block. `block_index`: the blocks of one slot carry 0 to ceil(cache_length / 512) - 1, each once; free blocks carry 0. `kv_cache`: keys may be large in a few tokens.
All inputs are finite; a program needn't handle non-finite values.
Results may differ from the reference program's by a relative error of at most 0.0061.
Values may be sent and summed in bfloat16 or wider, within the bound.
No kernel may reach another device: no remote copies, remote signals or barrier semaphores. Data moves between devices by JAX's collectives and lax.ppermute only.
A program may use at most 128 MiB of HBM per device.

```python
import jax
import jax.numpy as jnp
from jax import lax

D = 1280
HEADS = 16
HD = 80
FF = 1280
BLOCK = 512
RQ = 256
NBLK = 352
MAXB = 64
N_REP = 2


def layout(key):
    layout_key = jax.random.fold_in(key, 7001)
    streams = jax.random.split(layout_key, 8)
    slots = jnp.arange(RQ, dtype=jnp.int32)
    home_pick = jax.random.randint(streams[0], (RQ,), 0, 3)
    home_slot = (home_pick >= 2).astype(jnp.int32)
    long_zero = jax.random.randint(streams[1], (), 0, RQ)
    long_one = (long_zero + 1 + jax.random.randint(streams[2], (), 0, RQ - 1)) % RQ
    home_slot = jnp.where(slots == long_zero, 0, home_slot)
    home_slot = jnp.where(slots == long_one, 1, home_slot).astype(jnp.int32)
    shift_draw = jax.random.randint(streams[3], (RQ,), 0, 24)
    spare_want = jnp.right_shift(jnp.full((RQ,), MAXB - 1, jnp.int32), shift_draw)
    extras = jnp.zeros((RQ,), jnp.int32)
    longest = [long_zero, long_one]
    for replica in range(2):
        homed_here = home_slot == replica
        headroom = NBLK - jnp.sum(homed_here.astype(jnp.int32)) - (MAXB - 1)
        wanted = jnp.where(homed_here & (slots != longest[replica]), spare_want, 0)
        before = jnp.cumsum(wanted) - wanted
        granted = jnp.clip(headroom - before, 0, wanted)
        extras = extras + granted + jnp.where(slots == longest[replica], MAXB - 1, 0)
    counts = 1 + extras
    tail_tokens = jax.random.randint(streams[4], (RQ,), 1, BLOCK + 1)
    lengths = (counts - 1) * BLOCK + tail_tokens
    lengths = jnp.where((slots == long_zero) | (slots == long_one), MAXB * BLOCK, lengths).astype(jnp.int32)
    owner_rows = []
    index_rows = []
    sequence_pos = jnp.arange(NBLK, dtype=jnp.int32)
    for replica in range(2):
        sizes_here = jnp.where(home_slot == replica, counts, 0)
        run_ends = jnp.cumsum(sizes_here)
        run_starts = run_ends - sizes_here
        owner_seq = jnp.sum((run_ends[None, :] <= sequence_pos[:, None]).astype(jnp.int32), axis=1)
        index_seq = jnp.where(owner_seq < RQ, sequence_pos - run_starts[jnp.minimum(owner_seq, RQ - 1)], 0)
        source_pos = jax.random.permutation(streams[5 + replica], sequence_pos).astype(jnp.int32)
        owner_rows.append(owner_seq[source_pos])
        index_rows.append(index_seq[source_pos])
    return (home_slot, lengths, jnp.stack(owner_rows).astype(jnp.int32), jnp.stack(index_rows).astype(jnp.int32))


def draw_home_replica(key, part):
    return layout(key)[0]


def draw_cache_length(key, part):
    return layout(key)[1]


def draw_block_owner(key, part):
    return layout(key)[2]


def draw_block_index(key, part):
    return layout(key)[3]


def draw_kv_cache(key, part):
    total_blocks = N_REP * NBLK

    def one_block(block_number):
        block_key = jax.random.fold_in(key, block_number)
        streams = jax.random.split(block_key, 1)
        drawn_draw = jax.random.normal(streams[0], (BLOCK, HEADS, 2, HD), jnp.float32)
        drawn_draw = drawn_draw * jnp.array([2.0, 1.0], jnp.float32)[None, None, :, None]
        return drawn_draw.reshape(BLOCK, HEADS * 2 * HD).astype(jnp.bfloat16)
    drawn = lax.map(one_block, jnp.arange(total_blocks, dtype=jnp.int32))
    return drawn.reshape(N_REP, NBLK, BLOCK, HEADS * 2 * HD)


def plant(values, rng, least, top_value):
    longest = values.shape.index(max(values.shape))
    spots = []
    for shift in (0, 1):
        where = [jax.random.randint(jax.random.fold_in(rng, axis), (), 0, length) for axis, length in enumerate(values.shape)]
        where[longest] = (where[longest] + shift) % values.shape[longest]
        spots.append(tuple(where))
    return values.at[spots[0]].set(least).at[spots[1]].set(top_value)


def shard_levels(own_key, extent, shards, least, high):
    def one(position, parts):
        heights = jax.random.uniform(jax.random.fold_in(jax.random.fold_in(own_key, 6), position), (parts,), jnp.float32, least / len(shards), high / len(shards))
        return jnp.repeat(jnp.exp(heights), extent[position] // parts).reshape((-1,) + (1,) * (len(extent) - position - 1))

    gain = one(*shards[0])
    for cut in shards[1:]:
        gain = gain * one(*cut)
    return gain


def scatter_about(own_key, extent, width, most, cuts=(), kind=jnp.bfloat16):
    values = width * jax.random.normal(own_key, extent, jnp.float32)
    if cuts:
        values = values * shard_levels(own_key, extent, cuts, -0.22, 0.18)
    return jnp.clip(values, -most, most).astype(kind)


def setup_inputs(seed: int = 0) -> dict:
    keys = jax.random.split(jax.random.key(seed), 14)
    return {
        "token_state": scatter_about(keys[0], (RQ, D), 1.0, 6.0, ((0, 32),)),
        "attn_gain": jnp.clip(1.0 + 0.18 * jax.random.normal(keys[1], (D,), jnp.float32), 0.1, 1.9),
        "qkv_weight": scatter_about(keys[2], (D, HEADS * 3 * HD), D ** -0.5, 0.15625, ((1, 4),)),
        "out_weight": scatter_about(keys[3], (HEADS * HD, D), (HEADS * HD) ** -0.5, 0.15625, ((0, 4),)),
        "mlp_gain": jnp.clip(1.0 + 0.18 * jax.random.normal(keys[4], (D,), jnp.float32), 0.1, 1.9),
        "up_weight": scatter_about(keys[5], (D, FF), D ** -0.5, 0.15625, ((1, 4),)),
        "down_weight": scatter_about(keys[6], (FF, D), FF ** -0.5, 0.15625, ((0, 4),)),
        "kv_cache": draw_kv_cache(jax.random.fold_in(keys[13], 71), 0),
        "home_replica": draw_home_replica(jax.random.fold_in(keys[13], 71), 0),
        "moving": plant((jax.random.randint(keys[9], (RQ,), 0, 4) < 1).astype(jnp.int32), jax.random.fold_in(keys[9], 1), 0, 1),
        "cache_length": draw_cache_length(jax.random.fold_in(keys[13], 71), 0),
        "block_owner": draw_block_owner(jax.random.fold_in(keys[13], 71), 0),
        "block_index": draw_block_index(jax.random.fold_in(keys[13], 71), 0),
    }


very_low = -1e+30
norm_eps = 1e-06

def root_norm(values_in, gain_vector):
    values_in = values_in.astype(jnp.float32)
    scaled = values_in * lax.rsqrt(lax.optimization_barrier(jnp.mean(values_in * values_in, axis=-1, keepdims=True)) + norm_eps)
    return scaled * gain_vector

def reference(token_state, attn_gain, qkv_weight, out_weight, mlp_gain, up_weight, down_weight, kv_cache, home_replica, moving, cache_length, block_owner, block_index):
    requests = token_state.shape[0]
    normed = root_norm(token_state, attn_gain).astype(jnp.bfloat16)
    projected = jnp.dot(normed, qkv_weight, preferred_element_type=jnp.float32).reshape(requests, HEADS, 3, HD)
    query = (projected[:, :, 0] * HD ** (-0.5)).astype(jnp.bfloat16)
    fresh_pairs = projected[:, :, 1:].astype(jnp.bfloat16)
    block_count = N_REP * NBLK
    blocks = kv_cache.reshape(block_count, BLOCK, HEADS, 2, HD)
    owners = block_owner.reshape(block_count)
    block_starts = block_index.reshape(block_count)
    is_owned = owners < requests
    clipped = jnp.minimum(owners, requests - 1).astype(jnp.int32)
    offsets = jnp.arange(BLOCK, dtype=jnp.int32)

    def score_block(packed):
        cache_block, owner_slot, block_start, owned_here = packed
        raw_scores = jnp.einsum('hd,thd->th', query[owner_slot].astype(jnp.float32), cache_block[:, :, 0].astype(jnp.float32), precision=lax.Precision.HIGHEST)
        usable = owned_here & (block_start * BLOCK + offsets < cache_length[owner_slot])
        return (jnp.where(usable[:, None], raw_scores, very_low), usable)
    scores, usable = lax.map(score_block, (blocks, clipped, block_starts, is_owned))
    self_score = lax.optimization_barrier(jnp.sum(query.astype(jnp.float32) * fresh_pairs[:, :, 0].astype(jnp.float32), axis=-1))
    block_peak = lax.optimization_barrier(jnp.max(scores, axis=1))
    onehot = (clipped[:, None] == jnp.arange(requests, dtype=jnp.int32)[None, :]) & is_owned[:, None]
    cache_peak = lax.optimization_barrier(jnp.max(jnp.where(onehot[:, :, None], block_peak[:, None, :], very_low), axis=0))
    top_score = jnp.maximum(cache_peak, self_score)

    def weigh_block(packed):
        cache_block, block_scores, block_usable, owner_slot = packed
        weights = jnp.where(block_usable[:, None], jnp.exp(block_scores - top_score[owner_slot][None, :]), 0.0)
        block_total = lax.optimization_barrier(jnp.sum(weights, axis=0))
        rounded = lax.optimization_barrier(weights.astype(jnp.bfloat16))
        block_acc = jnp.einsum('th,thd->hd', rounded.astype(jnp.float32), cache_block[:, :, 1].astype(jnp.float32), precision=lax.Precision.HIGHEST)
        return (block_total, block_acc)
    totals, accums = lax.map(weigh_block, (blocks, scores, usable, clipped))
    selector = onehot.astype(jnp.float32)
    cache_total = jnp.einsum('bq,bh->qh', selector, totals, precision=lax.Precision.HIGHEST)
    cache_acc = jnp.einsum('bq,bhd->qhd', selector, accums, precision=lax.Precision.HIGHEST)
    self_weight = jnp.exp(self_score - top_score)
    rounded_self = lax.optimization_barrier(self_weight.astype(jnp.bfloat16)).astype(jnp.float32)
    denominator = cache_total + self_weight
    numerator = cache_acc + rounded_self[..., None] * fresh_pairs[:, :, 1].astype(jnp.float32)
    attended = (numerator / denominator[..., None]).astype(jnp.bfloat16).reshape(requests, HEADS * HD)
    residual = token_state.astype(jnp.float32) + jnp.dot(attended, out_weight, preferred_element_type=jnp.float32)
    normed_mlp = root_norm(residual, mlp_gain).astype(jnp.bfloat16)
    activated = jax.nn.gelu(jnp.dot(normed_mlp, up_weight, preferred_element_type=jnp.float32), approximate=True).astype(jnp.bfloat16)
    result = residual + jnp.dot(activated, down_weight, preferred_element_type=jnp.float32)
    target = jnp.bitwise_xor(home_replica, moving)
    replicas = jnp.arange(N_REP, dtype=jnp.int32)
    served = target[None, :] == replicas[:, None]
    hidden_out = jnp.where(served[:, :, None], result[None], jnp.zeros_like(result)[None])
    entries = projected[:, :, 1:].reshape(requests, HEADS * 2 * HD)
    new_entries = jnp.where(served[:, :, None], entries[None], jnp.zeros_like(entries)[None])
    return (hidden_out, new_entries)
```

```python
import functools

import jax
import jax.numpy as jnp
from jax import lax
from jax.experimental import pallas as pl
from jax.experimental.pallas import tpu as pltpu
from jax.sharding import PartitionSpec as P

HD = 80
PAIR = 2 * HD
VERY_LOW = -1e30
NORM_EPS = 1e-06
STATS = 320
WIDE = 384
F32 = jnp.float32
BF16 = jnp.bfloat16

VMEM = pl.BlockSpec(memory_space=pltpu.VMEM)
SMEM = pl.BlockSpec(memory_space=pltpu.SMEM)
PARAMS = pltpu.CompilerParams(vmem_limit_bytes=48 * 1024 * 1024)


def iota(shape, axis):
    return lax.broadcasted_iota(jnp.int32, shape, axis)


def root_norm(values, gain):
    mean = jnp.mean(values * values, axis=-1, keepdims=True)
    return values * lax.rsqrt(mean + NORM_EPS) * gain


def row_values(ref, start, rows, lanes):
    row = iota((rows, lanes), 0)
    out = jnp.zeros((rows, lanes), jnp.int32)
    for r in range(rows):
        out = jnp.where(row == r, ref[start + r], out)
    return out


def split3(value):
    high = value.astype(BF16).astype(F32)
    rest = value - high
    middle = rest.astype(BF16).astype(F32)
    return high, middle, (rest - middle).astype(BF16).astype(F32)


def project_kernel(place, home, moving, token, gain, weight, spread, query, fresh, entries):
    rows = token.shape[0]
    heads = weight.shape[1] // (3 * HD)
    normed = root_norm(token[...].astype(F32), gain[...]).astype(BF16)
    projected = jnp.dot(normed, weight[...], preferred_element_type=F32)
    own = jnp.concatenate(
        [projected[:, h * 3 * HD : h * 3 * HD + HD] for h in range(heads)]
        + [jnp.zeros((rows, WIDE - heads * HD), F32)],
        axis=1,
    )
    own = (own * HD ** (-0.5)).astype(BF16)
    query[...] = own
    for copy in range(spread.shape[0] // rows):
        spread[copy * rows : (copy + 1) * rows, :] = own
    pairs = jnp.concatenate(
        [projected[:, h * 3 * HD + HD : (h + 1) * 3 * HD] for h in range(heads)], axis=1
    )
    fresh[...] = pairs
    start = place[1] * rows
    target = row_values(home, start, rows, pairs.shape[1]) ^ row_values(
        moving, start, rows, pairs.shape[1]
    )
    entries[...] = jnp.where(target == place[0], pairs, 0.0)


def attend_kernel(owner, index, length, queries, cache, out, buffer, scores, sums, sems):
    blocks, tokens, width = cache.shape
    heads = width // PAIR
    requests = queries.shape[0]
    rows = sums.shape[0]
    copies = [
        pltpu.make_async_copy(cache.at[b], buffer.at[b], sems.at[b]) for b in range(blocks)
    ]
    for copy in copies:
        copy.start()
    row = iota((rows, 1), 0)
    owners = jnp.full((rows, 1), requests, jnp.int32)
    for b in range(blocks):
        owners = jnp.where(row == b, owner[0, b], owners)
    onehot = (iota((rows, requests), 1) == owners).astype(BF16)
    picked = jnp.dot(onehot, queries[...], preferred_element_type=F32)
    picked = jnp.concatenate([picked, jnp.zeros((rows, width - WIDE), F32)], axis=1)
    lane = iota((rows, width), 1)
    spread = jnp.zeros((rows, width), F32)
    for h in range(heads):
        moved = picked if h == 0 else pltpu.roll(picked, HD * h, 1)
        spread = jnp.where((lane >= PAIR * h) & (lane < PAIR * h + HD), moved, spread)
    head_lane = iota((8, width), 1) - PAIR * iota((8, width), 0)
    key_lanes = (head_lane >= 0) & (head_lane < HD)
    value_lanes = (head_lane >= HD) & (head_lane < PAIR)
    usable = []
    peaks = []
    for b in range(blocks):
        ask = jnp.where(key_lanes, jnp.broadcast_to(spread[b : b + 1], (8, width)), 0.0)
        copies[b].wait()
        score = lax.dot_general(
            ask.astype(BF16), buffer[b], (((1,), (1,)), ((), ())), preferred_element_type=F32
        )
        holder = owner[0, b]
        most = jnp.where(holder < requests, length[jnp.minimum(holder, requests - 1)], 0)
        use = iota((8, tokens), 1) < most - index[0, b] * tokens
        score = jnp.where(use, score, VERY_LOW)
        scores[b] = score
        usable.append(use)
        peaks.append(jnp.max(score, axis=1, keepdims=True))
    joint = []
    for b in range(blocks):
        peak = peaks[b]
        for c in range(blocks):
            if c != b:
                peak = jnp.maximum(peak, jnp.where(owner[0, c] == owner[0, b], peaks[c], VERY_LOW))
        joint.append(peak)
    stat_lane = iota((8, 128), 1) - (STATS - 256)
    stat_row = iota((8, 128), 0)
    stats = []
    for b in range(blocks):
        weights = jnp.where(usable[b], jnp.exp(scores[b] - joint[b]), 0.0)
        total = jnp.sum(weights, axis=1, keepdims=True)
        acc = jnp.dot(weights.astype(BF16), buffer[b], preferred_element_type=F32)
        sums[b : b + 1, :] = jnp.sum(jnp.where(value_lanes, acc, 0.0), axis=0, keepdims=True)
        stat = jnp.where(stat_lane == stat_row, joint[b], 0.0)
        stat = stat + jnp.where(stat_lane == stat_row + 8, total, 0.0)
        stats.append(jnp.sum(jnp.where(stat_row < heads, stat, 0.0), axis=0, keepdims=True))
    stats += [jnp.zeros((1, 128), F32)] * (rows - blocks)
    stats = jnp.concatenate(stats, axis=0)
    sums[blocks:rows, :] = jnp.zeros((rows - blocks, width), F32)
    packed = jnp.zeros((rows, width), F32)
    every = sums[...]
    for h in range(heads):
        moved = pltpu.roll(every, width - HD * (h + 1), 1)
        packed = jnp.where((lane >= HD * h) & (lane < HD * (h + 1)), moved, packed)
    packed = packed[:, :WIDE]
    added = jnp.zeros((rows, WIDE), F32)
    totals = jnp.zeros((rows, 128), F32)
    first = row < blocks
    for b in range(blocks):
        same = owners == owner[0, b]
        added = added + jnp.where(same, packed[b : b + 1], 0.0)
        totals = totals + jnp.where(same, stats[b : b + 1], 0.0)
        first = first & ((row <= b) | ~same)
    tail = iota((rows, 128), 1) - (STATS - 256)
    peak_part = jnp.where((tail >= 0) & (tail < 8), stats, 0.0)
    total_part = jnp.where((tail >= 8) & (tail < 16), totals, 0.0)
    parts = jnp.zeros((rows, 128), F32)
    for k, part in enumerate(split3(peak_part)):
        parts = parts + (part if k == 0 else pltpu.roll(part, 16 * k, 1))
    for k, part in enumerate(split3(total_part)):
        parts = parts + (part if k == 0 else pltpu.roll(part, 16 * k, 1))
    last = jnp.where(tail >= 0, parts, added[:, 256:])
    full = jnp.concatenate([added[:, :256], last], axis=1)
    full = jnp.where(first, full, 0.0).astype(BF16)
    place = (iota((rows, requests), 1) == owners) & first
    out[...] = lax.dot_general(
        place.astype(F32).astype(BF16),
        full,
        (((0,), (0,)), ((), ())),
        preferred_element_type=F32,
    ).astype(BF16)


def merge_kernel(shares, query, fresh, attended):
    rows = query.shape[0]
    count = shares.shape[0] // rows
    heads = fresh.shape[1] // PAIR
    sums = shares[...].astype(F32)
    tail = sums[:, 256:]
    joined = tail + pltpu.roll(tail, 128 - 16, 1) + pltpu.roll(tail, 128 - 32, 1)
    totals = pltpu.roll(joined, 128 - 8, 1)
    lane = iota(joined.shape, 1) - (STATS - 256)
    peaks = jnp.where((lane >= 0) & (lane < heads) & (totals > 0.0), joined, VERY_LOW)
    pair = fresh[...].astype(BF16).astype(F32)
    own = query[...].astype(F32)
    keys = jnp.concatenate([pair[:, PAIR * h : PAIR * h + HD] for h in range(heads)], axis=1)
    values = jnp.concatenate(
        [pair[:, PAIR * h + HD : PAIR * (h + 1)] for h in range(heads)], axis=1
    )
    product = own[:, : heads * HD] * keys
    head_of = iota((rows, heads * HD), 1) // HD
    own_lane = iota((rows, 128), 1) - (STATS - 256)
    self_score = jnp.full((rows, 128), VERY_LOW, F32)
    for h in range(heads):
        score = jnp.sum(jnp.where(head_of == h, product, 0.0), axis=1, keepdims=True)
        self_score = jnp.where(own_lane == h, score, self_score)
    top = self_score
    for s in range(count):
        top = jnp.maximum(top, peaks[s * rows : (s + 1) * rows])
    denominator = jnp.exp(self_score - top)
    self_weight = denominator.astype(BF16).astype(F32)
    wide_of = iota((rows, WIDE), 1) // HD

    def per_head(value):
        out = jnp.zeros((rows, WIDE), F32)
        for h in range(heads):
            at = STATS - 256 + h
            out = jnp.where(wide_of == h, value[:, at : at + 1], out)
        return out

    values = jnp.concatenate([values, jnp.zeros((rows, WIDE - heads * HD), F32)], axis=1)
    numerator = per_head(self_weight) * values
    for s in range(count):
        at = slice(s * rows, (s + 1) * rows)
        factor = jnp.exp(peaks[at] - top)
        denominator = denominator + factor * totals[at]
        numerator = numerator + per_head(factor) * sums[at]
    result = numerator / jnp.where(wide_of < heads, per_head(denominator), 1.0)
    attended[...] = result.astype(BF16)


def out_kernel(place, home, here, there, weight, partial):
    rows = here.shape[0]
    stay = row_values(home, place[1] * rows, rows, here.shape[1]) == place[0]
    attended = jnp.where(stay, here[...].astype(F32), there[...].astype(F32)).astype(BF16)
    partial[...] = jnp.dot(
        attended[:, : weight.shape[0]], weight[...], preferred_element_type=F32
    )


def hidden_kernel(token, own, left, right, across, gain, up, down, residual, partial):
    total = (own[...] + across[...]) + (left[...] + right[...])
    value = token[...].astype(F32) + total
    residual[...] = value
    normed = root_norm(value, gain[...]).astype(BF16)
    hidden = jnp.dot(normed, up[...], preferred_element_type=F32)
    active = jax.nn.gelu(hidden, approximate=True).astype(BF16)
    partial[...] = jnp.dot(active, down[...], preferred_element_type=F32)


def finish_kernel(place, home, moving, residual, own, left, right, across, out):
    rows = residual.shape[0]
    start = place[1] * rows
    result = residual[...] + ((own[...] + across[...]) + (left[...] + right[...]))
    target = row_values(home, start, rows, result.shape[1]) ^ row_values(
        moving, start, rows, result.shape[1]
    )
    out[...] = jnp.where(target == place[0], result, 0.0)


def shape(dims, dtype):
    return jax.ShapeDtypeStruct(dims, dtype)


def shifted(value, by):
    axes = ("rep", "tp")
    count = lax.axis_size("rep") * lax.axis_size("tp")
    return lax.ppermute(value, axes, [(i, (i + by) % count) for i in range(count)])


def from_ring(value):
    return shifted(value, 1), shifted(value, -1), shifted(value, 2)


def body(
    token_state,
    attn_gain,
    qkv_weight,
    out_weight,
    mlp_gain,
    up_weight,
    down_weight,
    kv_cache,
    home_replica,
    moving,
    cache_length,
    block_owner,
    block_index,
):
    rows, features = token_state.shape
    requests = home_replica.shape[0]
    _, blocks, tokens, width = kv_cache.shape
    place = jnp.stack([lax.axis_index("rep"), lax.axis_index("kv")]).astype(jnp.int32)

    spread, query, fresh, entries = pl.pallas_call(
        project_kernel,
        out_shape=(
            shape((requests, WIDE), BF16),
            shape((rows, WIDE), BF16),
            shape((rows, width), F32),
            shape((rows, width), F32),
        ),
        in_specs=[SMEM] * 3 + [VMEM] * 3,
        out_specs=(VMEM,) * 4,
        compiler_params=PARAMS,
        name="project",
    )(place, home_replica, moving, token_state, attn_gain[None], qkv_weight)
    queries = lax.all_to_all(spread, "kv", 0, 0, tiled=True)

    padded = -(-blocks // 16) * 16
    shares = pl.pallas_call(
        attend_kernel,
        out_shape=shape((requests, WIDE), BF16),
        in_specs=[SMEM] * 3 + [VMEM, pl.BlockSpec(memory_space=pl.ANY)],
        out_specs=VMEM,
        scratch_shapes=[
            pltpu.VMEM((blocks, tokens, width), BF16),
            pltpu.VMEM((blocks, 8, tokens), F32),
            pltpu.VMEM((padded, width), F32),
            pltpu.SemaphoreType.DMA((blocks,)),
        ],
        compiler_params=PARAMS,
        name="attend",
    )(block_owner, block_index, cache_length, queries, kv_cache[0])
    shares = lax.all_to_all(shares, "kv", 0, 0, tiled=True)

    attended = pl.pallas_call(
        merge_kernel,
        out_shape=shape((rows, WIDE), BF16),
        in_specs=[VMEM] * 3,
        out_specs=VMEM,
        compiler_params=PARAMS,
        name="merge",
    )(shares, query, fresh)
    other = lax.ppermute(attended, "rep", [(0, 1), (1, 0)])

    partial = pl.pallas_call(
        out_kernel,
        out_shape=shape((rows, features), F32),
        in_specs=[SMEM] * 2 + [VMEM] * 3,
        out_specs=VMEM,
        compiler_params=PARAMS,
        name="out_projection",
    )(place, home_replica, attended, other, out_weight)
    residual, partial = pl.pallas_call(
        hidden_kernel,
        out_shape=(shape((rows, features), F32),) * 2,
        in_specs=[VMEM] * 8,
        out_specs=(VMEM,) * 2,
        compiler_params=PARAMS,
        name="hidden",
    )(token_state, partial, *from_ring(partial), mlp_gain[None], up_weight, down_weight)
    result = pl.pallas_call(
        finish_kernel,
        out_shape=shape((rows, features), F32),
        in_specs=[SMEM] * 3 + [VMEM] * 5,
        out_specs=VMEM,
        compiler_params=PARAMS,
        name="finish",
    )(place, home_replica, moving, residual, partial, *from_ring(partial))
    return (result[None], entries[None])


def solution(mesh):
    return jax.shard_map(
        body,
        mesh=mesh,
        in_specs=(
            P("kv", None),
            P(),
            P(None, "tp"),
            P("tp", None),
            P(),
            P(None, "tp"),
            P("tp", None),
            P("rep", "kv", None, "tp"),
            P(),
            P(),
            P(),
            P("rep", "kv"),
            P("rep", "kv"),
        ),
        out_specs=(P("rep", "kv", None), P("rep", "kv", "tp")),
        check_vma=False,
    )
```

```python
import functools

import jax
import jax.numpy as jnp
from jax import lax
from jax.experimental import pallas as pl
from jax.experimental.pallas import tpu as pltpu
from jax.sharding import PartitionSpec as P

HD = 80
PAIR = 2 * HD
VERY_LOW = -1e30
NORM_EPS = 1e-06
STATS = 320
WIDE = 384
F32 = jnp.float32
BF16 = jnp.bfloat16

VMEM = pl.BlockSpec(memory_space=pltpu.VMEM)
SMEM = pl.BlockSpec(memory_space=pltpu.SMEM)
PARAMS = pltpu.CompilerParams(vmem_limit_bytes=16 * 1024 * 1024)


def iota(shape, axis):
    return lax.broadcasted_iota(jnp.int32, shape, axis)


def root_norm(values, gain):
    mean = jnp.mean(values * values, axis=-1, keepdims=True)
    return values * lax.rsqrt(mean + NORM_EPS) * gain


def row_values(ref, start, rows, lanes):
    row = iota((rows, lanes), 0)
    out = jnp.zeros((rows, lanes), jnp.int32)
    for r in range(rows):
        out = jnp.where(row == r, ref[start + r], out)
    return out


def widen(value, lanes):
    return jnp.concatenate([value] * (lanes // value.shape[1]), axis=1)


def split3(value):
    high = value.astype(BF16).astype(F32)
    rest = value - high
    middle = rest.astype(BF16).astype(F32)
    return high, middle, (rest - middle).astype(BF16).astype(F32)


def dot_transposed(left, right):
    return lax.dot_general(left, right, (((1,), (1,)), ((), ())), preferred_element_type=F32)


def project_kernel(
    place, home, moving, token, gain, weight, spread, query, fresh, entries, homed, served
):
    rows = token.shape[0]
    heads = weight.shape[0] // (3 * HD)
    normed = root_norm(token[...].astype(F32), gain[...]).astype(BF16)
    projected = dot_transposed(normed, weight[...])
    own = jnp.concatenate(
        [projected[:, h * 3 * HD : h * 3 * HD + HD] for h in range(heads)]
        + [jnp.zeros((rows, WIDE - heads * HD), F32)],
        axis=1,
    )
    own = (own * HD ** (-0.5)).astype(BF16)
    query[...] = own
    for copy in range(spread.shape[0] // rows):
        spread[copy * rows : (copy + 1) * rows, :] = own
    pairs = jnp.concatenate(
        [projected[:, h * 3 * HD + HD : (h + 1) * 3 * HD] for h in range(heads)], axis=1
    )
    fresh[...] = pairs
    start = place[1] * rows
    at_home = row_values(home, start, rows, 128)
    target = at_home ^ row_values(moving, start, rows, 128)
    homed[...] = jnp.where(at_home == place[0], 1.0, 0.0)
    serves = jnp.where(target == place[0], 1.0, 0.0)
    served[...] = serves
    entries[...] = jnp.where(widen(serves, pairs.shape[1]) > 0.0, pairs, 0.0)


def attend_kernel(owner, index, length, queries, cache, out, scores, sums):
    blocks, tokens, width = cache.shape
    heads = width // PAIR
    requests = queries.shape[0]
    rows = sums.shape[0]
    row = iota((rows, 1), 0)
    owners = jnp.full((rows, 1), requests, jnp.int32)
    for b in range(blocks):
        owners = jnp.where(row == b, owner[0, b], owners)
    onehot = (iota((rows, requests), 1) == owners).astype(BF16)
    picked = jnp.dot(onehot, queries[...], preferred_element_type=F32)
    picked = jnp.concatenate([picked, jnp.zeros((rows, width - WIDE), F32)], axis=1)
    lane = iota((rows, width), 1)
    spread = jnp.zeros((rows, width), F32)
    for h in range(heads):
        moved = picked if h == 0 else pltpu.roll(picked, HD * h, 1)
        spread = jnp.where((lane >= PAIR * h) & (lane < PAIR * h + HD), moved, spread)
    head_lane = iota((8, width), 1) - PAIR * iota((8, width), 0)
    key_lanes = (head_lane >= 0) & (head_lane < HD)
    value_lanes = (head_lane >= HD) & (head_lane < PAIR)
    usable = []
    peaks = []
    for b in range(blocks):
        ask = jnp.where(key_lanes, jnp.broadcast_to(spread[b : b + 1], (8, width)), 0.0)
        score = dot_transposed(ask.astype(BF16), cache[b])
        holder = owner[0, b]
        most = jnp.where(holder < requests, length[jnp.minimum(holder, requests - 1)], 0)
        use = iota((8, tokens), 1) < most - index[0, b] * tokens
        score = jnp.where(use, score, VERY_LOW)
        scores[b] = score
        usable.append(use)
        peaks.append(jnp.max(score, axis=1, keepdims=True))
    joint = []
    for b in range(blocks):
        peak = peaks[b]
        for c in range(blocks):
            if c != b:
                peak = jnp.maximum(peak, jnp.where(owner[0, c] == owner[0, b], peaks[c], VERY_LOW))
        joint.append(peak)
    stat_lane = iota((8, 128), 1) - (STATS - 256)
    stat_row = iota((8, 128), 0)
    stats = []
    for b in range(blocks):
        weights = jnp.where(usable[b], jnp.exp(scores[b] - joint[b]), 0.0)
        total = jnp.sum(weights, axis=1, keepdims=True)
        acc = jnp.dot(weights.astype(BF16), cache[b], preferred_element_type=F32)
        sums[b : b + 1, :] = jnp.sum(jnp.where(value_lanes, acc, 0.0), axis=0, keepdims=True)
        stat = jnp.where(stat_lane == stat_row, joint[b], 0.0)
        stat = stat + jnp.where(stat_lane == stat_row + 8, total, 0.0)
        stats.append(jnp.sum(jnp.where(stat_row < heads, stat, 0.0), axis=0, keepdims=True))
    stats += [jnp.zeros((1, 128), F32)] * (rows - blocks)
    stats = jnp.concatenate(stats, axis=0)
    sums[blocks:rows, :] = jnp.zeros((rows - blocks, width), F32)
    packed = jnp.zeros((rows, width), F32)
    every = sums[...]
    for h in range(heads):
        moved = pltpu.roll(every, width - HD * (h + 1), 1)
        packed = jnp.where((lane >= HD * h) & (lane < HD * (h + 1)), moved, packed)
    packed = packed[:, :WIDE]
    added = jnp.zeros((rows, WIDE), F32)
    totals = jnp.zeros((rows, 128), F32)
    first = row < blocks
    for b in range(blocks):
        same = owners == owner[0, b]
        added = added + jnp.where(same, packed[b : b + 1], 0.0)
        totals = totals + jnp.where(same, stats[b : b + 1], 0.0)
        first = first & ((row <= b) | ~same)
    tail = iota((rows, 128), 1) - (STATS - 256)
    peak_part = jnp.where((tail >= 0) & (tail < 8), stats, 0.0)
    total_part = jnp.where((tail >= 8) & (tail < 16), totals, 0.0)
    parts = jnp.zeros((rows, 128), F32)
    for k, part in enumerate(split3(peak_part)):
        parts = parts + (part if k == 0 else pltpu.roll(part, 16 * k, 1))
    for k, part in enumerate(split3(total_part)):
        parts = parts + (part if k == 0 else pltpu.roll(part, 16 * k, 1))
    last = jnp.where(tail >= 0, parts, added[:, 256:])
    full = jnp.concatenate([added[:, :256], last], axis=1)
    full = jnp.where(first, full, 0.0).astype(BF16)
    place = (iota((rows, requests), 1) == owners) & first
    out[...] = lax.dot_general(
        place.astype(F32).astype(BF16),
        full,
        (((0,), (0,)), ((), ())),
        preferred_element_type=F32,
    ).astype(BF16)


def merge_kernel(shares, query, fresh, homed, weight, spread):
    rows = query.shape[0]
    count = shares.shape[0] // rows
    heads = fresh.shape[1] // PAIR
    sums = shares[...].astype(F32)
    tail = sums[:, 256:]
    joined = tail + pltpu.roll(tail, 128 - 16, 1) + pltpu.roll(tail, 128 - 32, 1)
    totals = pltpu.roll(joined, 128 - 8, 1)
    lane = iota(joined.shape, 1) - (STATS - 256)
    peaks = jnp.where((lane >= 0) & (lane < heads) & (totals > 0.0), joined, VERY_LOW)
    pair = fresh[...].astype(BF16).astype(F32)
    own = query[...].astype(F32)
    keys = jnp.concatenate([pair[:, PAIR * h : PAIR * h + HD] for h in range(heads)], axis=1)
    values = jnp.concatenate(
        [pair[:, PAIR * h + HD : PAIR * (h + 1)] for h in range(heads)], axis=1
    )
    product = own[:, : heads * HD] * keys
    head_of = iota((rows, heads * HD), 1) // HD
    own_lane = iota((rows, 128), 1) - (STATS - 256)
    self_score = jnp.full((rows, 128), VERY_LOW, F32)
    for h in range(heads):
        score = jnp.sum(jnp.where(head_of == h, product, 0.0), axis=1, keepdims=True)
        self_score = jnp.where(own_lane == h, score, self_score)
    top = self_score
    for s in range(count):
        top = jnp.maximum(top, peaks[s * rows : (s + 1) * rows])
    denominator = jnp.exp(self_score - top)
    self_weight = denominator.astype(BF16).astype(F32)
    wide_of = iota((rows, WIDE), 1) // HD

    def per_head(value):
        out = jnp.zeros((rows, WIDE), F32)
        for h in range(heads):
            at = STATS - 256 + h
            out = jnp.where(wide_of == h, value[:, at : at + 1], out)
        return out

    values = jnp.concatenate([values, jnp.zeros((rows, WIDE - heads * HD), F32)], axis=1)
    numerator = per_head(self_weight) * values
    for s in range(count):
        at = slice(s * rows, (s + 1) * rows)
        factor = jnp.exp(peaks[at] - top)
        denominator = denominator + factor * totals[at]
        numerator = numerator + per_head(factor) * sums[at]
    result = numerator / jnp.where(wide_of < heads, per_head(denominator), 1.0)
    attended = jnp.where(widen(homed[...], WIDE) > 0.0, result, 0.0).astype(BF16)
    partial = jnp.dot(
        attended[:, : weight.shape[0]], weight[...], preferred_element_type=F32
    ).astype(BF16)
    for copy in range(spread.shape[0]):
        spread[copy] = partial


def hidden_kernel(token, shares, gain, up, down, residual, partial):
    total = token[...].astype(F32)
    for share in range(shares.shape[0]):
        total = total + shares[share].astype(F32)
    residual[...] = total
    normed = root_norm(total, gain[...]).astype(BF16)
    hidden = dot_transposed(normed, up[...])
    active = jax.nn.gelu(hidden, approximate=True).astype(BF16)
    partial[...] = jnp.dot(active, down[...], preferred_element_type=F32).astype(BF16)


def finish_kernel(served, residual, own, near, across, far, out):
    own, near, across, far = (v[...].astype(F32) for v in (own, near, across, far))
    result = residual[...] + ((own + near) + (across + far))
    out[...] = jnp.where(widen(served[...], result.shape[1]) > 0.0, result, 0.0)


def shape(dims, dtype):
    return jax.ShapeDtypeStruct(dims, dtype)


def from_others(value, axis):
    count = lax.axis_size(axis)
    return [
        lax.ppermute(value, axis, [(i, i ^ bits) for i in range(count)])
        for bits in range(1, count)
    ]


def body(
    token_state,
    attn_gain,
    qkv_weight,
    out_weight,
    mlp_gain,
    up_weight,
    down_weight,
    kv_cache,
    home_replica,
    moving,
    cache_length,
    block_owner,
    block_index,
):
    rows, features = token_state.shape
    requests = home_replica.shape[0]
    _, blocks, tokens, width = kv_cache.shape
    place = jnp.stack([lax.axis_index("rep"), lax.axis_index("kv")]).astype(jnp.int32)

    spread, query, fresh, entries, homed, served = pl.pallas_call(
        project_kernel,
        out_shape=(
            shape((requests, WIDE), BF16),
            shape((rows, WIDE), BF16),
            shape((rows, width), F32),
            shape((rows, width), F32),
            shape((rows, 128), F32),
            shape((rows, 128), F32),
        ),
        in_specs=[SMEM] * 3 + [VMEM] * 3,
        out_specs=(VMEM,) * 6,
        compiler_params=PARAMS,
        name="project",
    )(place, home_replica, moving, token_state, attn_gain[None], qkv_weight.T)
    queries = lax.all_to_all(spread, "kv", 0, 0, tiled=True)

    padded = -(-blocks // 16) * 16
    shares = pl.pallas_call(
        attend_kernel,
        out_shape=shape((requests, WIDE), BF16),
        in_specs=[SMEM] * 3 + [VMEM] * 2,
        out_specs=VMEM,
        scratch_shapes=[
            pltpu.VMEM((blocks, 8, tokens), F32),
            pltpu.VMEM((padded, width), F32),
        ],
        compiler_params=PARAMS,
        name="attend",
    )(block_owner, block_index, cache_length, queries, kv_cache[0])
    shares = lax.all_to_all(shares, "kv", 0, 0, tiled=True)

    everyone = ("rep", "tp")
    count = lax.axis_size("rep") * lax.axis_size("tp")
    partials = pl.pallas_call(
        merge_kernel,
        out_shape=shape((count, rows, features), BF16),
        in_specs=[VMEM] * 5,
        out_specs=VMEM,
        compiler_params=PARAMS,
        name="merge",
    )(shares, query, fresh, homed, out_weight)
    partials = lax.all_to_all(partials, everyone, 0, 0, tiled=True)

    residual, partial = pl.pallas_call(
        hidden_kernel,
        out_shape=(shape((rows, features), F32), shape((rows, features), BF16)),
        in_specs=[VMEM] * 5,
        out_specs=(VMEM,) * 2,
        compiler_params=PARAMS,
        name="hidden",
    )(token_state, partials, mlp_gain[None], up_weight.T, down_weight)
    result = pl.pallas_call(
        finish_kernel,
        out_shape=shape((rows, features), F32),
        in_specs=[VMEM] * 6,
        out_specs=VMEM,
        compiler_params=PARAMS,
        name="finish",
    )(served, residual, partial, *from_others(partial, "tp"))
    return (result[None], entries[None])


def solution(mesh):
    return jax.shard_map(
        body,
        mesh=mesh,
        in_specs=(
            P("kv", None),
            P(),
            P(None, "tp"),
            P("tp", None),
            P(),
            P(None, "tp"),
            P("tp", None),
            P("rep", "kv", None, "tp"),
            P(),
            P(),
            P(),
            P("rep", "kv"),
            P("rep", "kv"),
        ),
        out_specs=(P("rep", "kv", None), P("rep", "kv", "tp")),
        check_vma=False,
    )
```

```python
import functools

import jax
import jax.numpy as jnp
from jax import lax
from jax.experimental import pallas as pl
from jax.experimental.pallas import tpu as pltpu
from jax.sharding import PartitionSpec as P

HD = 80
PAIR = 2 * HD
VERY_LOW = -1e30
NORM_EPS = 1e-06
EARLY = 3
STATS = 320
WIDE = 384
F32 = jnp.float32
BF16 = jnp.bfloat16

VMEM = pl.BlockSpec(memory_space=pltpu.VMEM)
HBM = pl.BlockSpec(memory_space=pltpu.HBM)
SMEM = pl.BlockSpec(memory_space=pltpu.SMEM)
PARAMS = pltpu.CompilerParams(vmem_limit_bytes=16 * 1024 * 1024)


def in_hbm(*arrays):
    return [pltpu.with_memory_space_constraint(a, pltpu.HBM) for a in arrays]


def iota(shape, axis):
    return lax.broadcasted_iota(jnp.int32, shape, axis)


def root_norm(values, gain):
    mean = jnp.mean(values * values, axis=-1, keepdims=True)
    return values * lax.rsqrt(mean + NORM_EPS) * gain


def row_values(ref, start, rows, lanes):
    row = iota((rows, lanes), 0)
    out = jnp.zeros((rows, lanes), jnp.int32)
    for r in range(rows):
        out = jnp.where(row == r, ref[start + r], out)
    return out


def widen(value, lanes):
    return jnp.concatenate([value] * (lanes // value.shape[1]), axis=1)


def split3(value):
    high = value.astype(BF16).astype(F32)
    rest = value - high
    middle = rest.astype(BF16).astype(F32)
    return high, middle, (rest - middle).astype(BF16).astype(F32)


def dot_transposed(left, right):
    return lax.dot_general(left, right, (((1,), (1,)), ((), ())), preferred_element_type=F32)


def fetch(pairs, sems):
    copies = [pltpu.make_async_copy(a, b, sems.at[i]) for i, (a, b) in enumerate(pairs)]
    for copy in copies:
        copy.start()
    return copies


def project_kernel(
    token_hbm, gain_hbm, weight_hbm, spread, query, fresh, token, gain, weight, sems
):
    rows = token.shape[0]
    heads = weight.shape[0] // (3 * HD)
    copies = fetch(
        [(token_hbm, token), (gain_hbm, gain.at[0]), (weight_hbm, weight)], sems
    )
    copies[0].wait()
    copies[1].wait()
    normed = root_norm(token[...].astype(F32), gain[...]).astype(BF16)
    copies[2].wait()
    projected = dot_transposed(normed, weight[...])
    own = jnp.concatenate(
        [projected[:, h * 3 * HD : h * 3 * HD + HD] for h in range(heads)]
        + [jnp.zeros((rows, WIDE - heads * HD), F32)],
        axis=1,
    )
    own = (own * HD ** (-0.5)).astype(BF16)
    query[...] = own
    for copy in range(spread.shape[0] // rows):
        spread[copy * rows : (copy + 1) * rows, :] = own
    fresh[...] = jnp.concatenate(
        [projected[:, h * 3 * HD + HD : (h + 1) * 3 * HD] for h in range(heads)], axis=1
    )


def side_kernel(
    place,
    owner_hbm,
    index_hbm,
    length_hbm,
    home_hbm,
    moving_hbm,
    cache_hbm,
    fresh,
    cache,
    owners,
    remains,
    entries,
    homed,
    served,
    owner,
    index,
    length,
    home,
    moving,
    sems,
):
    rows = fresh.shape[0]
    blocks, tokens, _ = cache_hbm.shape
    requests = length.shape[0]
    copies = fetch(
        [
            (owner_hbm, owner),
            (index_hbm, index),
            (length_hbm, length),
            (home_hbm, home),
            (moving_hbm, moving),
            (cache_hbm.at[: cache.shape[0]], cache),
        ],
        sems,
    )
    for copy in copies[:5]:
        copy.wait()
    row = iota(owners.shape, 0)
    holders = jnp.full(owners.shape, requests, jnp.int32)
    left = jnp.zeros(owners.shape, jnp.int32)
    for b in range(blocks):
        holder = owner[0, b]
        most = jnp.where(holder < requests, length[jnp.minimum(holder, requests - 1)], 0)
        holders = jnp.where(row == b, holder, holders)
        left = jnp.where(row == b, most - index[0, b] * tokens, left)
    owners[...] = holders
    remains[...] = left
    start = place[1] * rows
    at_home = row_values(home, start, rows, 128)
    target = at_home ^ row_values(moving, start, rows, 128)
    homed[...] = jnp.where(at_home == place[0], 1.0, 0.0)
    serves = jnp.where(target == place[0], 1.0, 0.0)
    served[...] = serves
    pairs = fresh[...]
    entries[...] = jnp.where(widen(serves, pairs.shape[1]) > 0.0, pairs, 0.0)
    copies[5].wait()


def attend_kernel(
    owner_of, remains, queries, early, cache_hbm, out, late, scores, sums, sems
):
    blocks, tokens, width = cache_hbm.shape
    ready = early.shape[0]
    copies = fetch(
        [(cache_hbm.at[b], late.at[b - ready]) for b in range(ready, blocks)], sems
    )

    def cache(b):
        return early[b] if b < ready else late[b - ready]

    heads = width // PAIR
    requests = queries.shape[0]
    rows = sums.shape[0]
    onehot = (iota((rows, requests), 1) == widen(owner_of[...], requests)).astype(BF16)
    picked = jnp.dot(onehot, queries[...], preferred_element_type=F32)
    picked = jnp.concatenate([picked, jnp.zeros((rows, width - WIDE), F32)], axis=1)
    lane = iota((rows, width), 1)
    spread = jnp.zeros((rows, width), F32)
    for h in range(heads):
        moved = picked if h == 0 else pltpu.roll(picked, HD * h, 1)
        spread = jnp.where((lane >= PAIR * h) & (lane < PAIR * h + HD), moved, spread)
    head_lane = iota((8, width), 1) - PAIR * iota((8, width), 0)
    key_lanes = (head_lane >= 0) & (head_lane < HD)
    value_lanes = (head_lane >= HD) & (head_lane < PAIR)
    block_lane = iota((8, 128), 1)
    token_lane = iota((8, tokens), 1)
    every_peak = jnp.full((8, 128), VERY_LOW, F32)
    holders = jnp.full((8, 128), requests, jnp.int32)
    usable = []
    for b in range(blocks):
        ask = jnp.where(key_lanes, jnp.broadcast_to(spread[b : b + 1], (8, width)), 0.0)
        if b >= ready:
            copies[b - ready].wait()
        score = dot_transposed(ask.astype(BF16), cache(b))
        use = token_lane < widen(jnp.broadcast_to(remains[b : b + 1, :], (8, 128)), tokens)
        score = jnp.where(use, score, VERY_LOW)
        scores[b] = score
        usable.append(use)
        peak = jnp.max(score, axis=1, keepdims=True)
        every_peak = jnp.where(block_lane == b, peak, every_peak)
        holders = jnp.where(block_lane == b, owner_of[b : b + 1, :], holders)
    stat_lane = iota((8, 128), 1) - (STATS - 256)
    stat_row = iota((8, 128), 0)
    stats = []
    for b in range(blocks):
        peers = jnp.where(holders == owner_of[b : b + 1, :], every_peak, VERY_LOW)
        joint = jnp.max(peers, axis=1, keepdims=True)
        weights = jnp.where(usable[b], jnp.exp(scores[b] - joint), 0.0)
        total = jnp.sum(weights, axis=1, keepdims=True)
        acc = jnp.dot(weights.astype(BF16), cache(b), preferred_element_type=F32)
        sums[b : b + 1, :] = jnp.sum(jnp.where(value_lanes, acc, 0.0), axis=0, keepdims=True)
        stat = jnp.where(stat_lane == stat_row, joint, 0.0)
        stat = stat + jnp.where(stat_lane == stat_row + 8, total, 0.0)
        stats.append(jnp.sum(jnp.where(stat_row < heads, stat, 0.0), axis=0, keepdims=True))
    stats += [jnp.zeros((1, 128), F32)] * (rows - blocks)
    stats = jnp.concatenate(stats, axis=0)
    sums[blocks:rows, :] = jnp.zeros((rows - blocks, width), F32)
    packed = jnp.zeros((rows, width), F32)
    every = sums[...]
    for h in range(heads):
        moved = pltpu.roll(every, width - HD * (h + 1), 1)
        packed = jnp.where((lane >= HD * h) & (lane < HD * (h + 1)), moved, packed)
    packed = packed[:, :WIDE]
    added = jnp.zeros((rows, WIDE), F32)
    totals = jnp.zeros((rows, 128), F32)
    first = iota((rows, 128), 0) < blocks
    for b in range(blocks):
        same = owner_of[...] == owner_of[b : b + 1, :]
        added = added + jnp.where(widen(same, WIDE), packed[b : b + 1], 0.0)
        totals = totals + jnp.where(same, stats[b : b + 1], 0.0)
        first = first & ((iota((rows, 128), 0) <= b) | ~same)
    tail = iota((rows, 128), 1) - (STATS - 256)
    peak_part = jnp.where((tail >= 0) & (tail < 8), stats, 0.0)
    total_part = jnp.where((tail >= 8) & (tail < 16), totals, 0.0)
    parts = jnp.zeros((rows, 128), F32)
    for k, part in enumerate(split3(peak_part)):
        parts = parts + (part if k == 0 else pltpu.roll(part, 16 * k, 1))
    for k, part in enumerate(split3(total_part)):
        parts = parts + (part if k == 0 else pltpu.roll(part, 16 * k, 1))
    last = jnp.where(tail >= 0, parts, added[:, 256:])
    full = jnp.concatenate([added[:, :256], last], axis=1)
    keep = jnp.where(first, 1.0, 0.0)
    full = jnp.where(widen(keep, WIDE) > 0.0, full, 0.0).astype(BF16)
    out[...] = lax.dot_general(
        onehot,
        full,
        (((0,), (0,)), ((), ())),
        preferred_element_type=F32,
    ).astype(BF16)


def merge_kernel(shares, query, fresh, homed, weight, spread):
    rows = query.shape[0]
    count = shares.shape[0] // rows
    heads = fresh.shape[1] // PAIR
    sums = shares[...].astype(F32)
    tail = sums[:, 256:]
    joined = tail + pltpu.roll(tail, 128 - 16, 1) + pltpu.roll(tail, 128 - 32, 1)
    totals = pltpu.roll(joined, 128 - 8, 1)
    lane = iota(joined.shape, 1) - (STATS - 256)
    peaks = jnp.where((lane >= 0) & (lane < heads) & (totals > 0.0), joined, VERY_LOW)
    pair = fresh[...].astype(BF16).astype(F32)
    own = query[...].astype(F32)
    keys = jnp.concatenate([pair[:, PAIR * h : PAIR * h + HD] for h in range(heads)], axis=1)
    values = jnp.concatenate(
        [pair[:, PAIR * h + HD : PAIR * (h + 1)] for h in range(heads)], axis=1
    )
    product = own[:, : heads * HD] * keys
    head_of = iota((rows, heads * HD), 1) // HD
    own_lane = iota((rows, 128), 1) - (STATS - 256)
    self_score = jnp.full((rows, 128), VERY_LOW, F32)
    for h in range(heads):
        score = jnp.sum(jnp.where(head_of == h, product, 0.0), axis=1, keepdims=True)
        self_score = jnp.where(own_lane == h, score, self_score)
    top = self_score
    for s in range(count):
        top = jnp.maximum(top, peaks[s * rows : (s + 1) * rows])
    denominator = jnp.exp(self_score - top)
    self_weight = denominator.astype(BF16).astype(F32)
    wide_of = iota((rows, WIDE), 1) // HD

    def per_head(value):
        out = jnp.zeros((rows, WIDE), F32)
        for h in range(heads):
            at = STATS - 256 + h
            out = jnp.where(wide_of == h, value[:, at : at + 1], out)
        return out

    values = jnp.concatenate([values, jnp.zeros((rows, WIDE - heads * HD), F32)], axis=1)
    numerator = per_head(self_weight) * values
    for s in range(count):
        at = slice(s * rows, (s + 1) * rows)
        factor = jnp.exp(peaks[at] - top)
        denominator = denominator + factor * totals[at]
        numerator = numerator + per_head(factor) * sums[at]
    result = numerator / jnp.where(wide_of < heads, per_head(denominator), 1.0)
    attended = jnp.where(widen(homed[...], WIDE) > 0.0, result, 0.0).astype(BF16)
    partial = jnp.dot(
        attended[:, : weight.shape[0]], weight[...], preferred_element_type=F32
    ).astype(BF16)
    for copy in range(spread.shape[0]):
        spread[copy] = partial


def hidden_kernel(token, shares, gain, up, down, residual, partial):
    total = token[...].astype(F32)
    for share in range(shares.shape[0]):
        total = total + shares[share].astype(F32)
    residual[...] = total
    normed = root_norm(total, gain[...]).astype(BF16)
    hidden = dot_transposed(normed, up[...])
    active = jax.nn.gelu(hidden, approximate=True).astype(BF16)
    partial[...] = jnp.dot(active, down[...], preferred_element_type=F32).astype(BF16)


def finish_kernel(served, residual, own, near, across, far, out):
    own, near, across, far = (v[...].astype(F32) for v in (own, near, across, far))
    result = residual[...] + ((own + near) + (across + far))
    out[...] = jnp.where(widen(served[...], result.shape[1]) > 0.0, result, 0.0)


def shape(dims, dtype):
    return jax.ShapeDtypeStruct(dims, dtype)


def from_others(value, axis):
    count = lax.axis_size(axis)
    return [
        lax.ppermute(value, axis, [(i, i ^ bits) for i in range(count)])
        for bits in range(1, count)
    ]


def body(
    token_state,
    attn_gain,
    qkv_weight,
    out_weight,
    mlp_gain,
    up_weight,
    down_weight,
    kv_cache,
    home_replica,
    moving,
    cache_length,
    block_owner,
    block_index,
):
    rows, features = token_state.shape
    requests = home_replica.shape[0]
    _, blocks, tokens, width = kv_cache.shape
    place = jnp.stack([lax.axis_index("rep"), lax.axis_index("kv")]).astype(jnp.int32)

    spread, query, fresh = pl.pallas_call(
        project_kernel,
        out_shape=(
            shape((requests, WIDE), BF16),
            shape((rows, WIDE), BF16),
            shape((rows, width), F32),
        ),
        in_specs=[HBM] * 3,
        out_specs=(VMEM,) * 3,
        scratch_shapes=[
            pltpu.VMEM((rows, features), BF16),
            pltpu.VMEM((1, features), F32),
            pltpu.VMEM(qkv_weight.shape[::-1], BF16),
            pltpu.SemaphoreType.DMA((3,)),
        ],
        compiler_params=PARAMS,
        name="project",
    )(*in_hbm(token_state, attn_gain, qkv_weight.T))
    queries = lax.all_to_all(spread, "kv", 0, 0, tiled=True)

    padded = -(-blocks // 16) * 16
    early, owners, remains, entries, homed, served = pl.pallas_call(
        side_kernel,
        out_shape=(
            pltpu.VMEM((EARLY, tokens, width), BF16),
            shape((padded, 128), jnp.int32),
            shape((padded, 128), jnp.int32),
            shape((rows, width), F32),
            shape((rows, 128), F32),
            shape((rows, 128), F32),
        ),
        in_specs=[SMEM] + [HBM] * 6 + [VMEM],
        out_specs=(VMEM,) * 6,
        scratch_shapes=[pltpu.SMEM((1, blocks), jnp.int32)] * 2
        + [pltpu.SMEM((requests,), jnp.int32)] * 3
        + [pltpu.SemaphoreType.DMA((6,))],
        compiler_params=PARAMS,
        cost_estimate=pl.CostEstimate(
            flops=0, bytes_accessed=2 * EARLY * tokens * width * 2, transcendentals=0
        ),
        name="side",
    )(
        place,
        *in_hbm(
            block_owner, block_index, cache_length, home_replica, moving, kv_cache[0]
        ),
        fresh,
    )

    shares = pl.pallas_call(
        attend_kernel,
        out_shape=shape((requests, WIDE), BF16),
        in_specs=[VMEM] * 4 + [HBM],
        out_specs=VMEM,
        scratch_shapes=[
            pltpu.VMEM((blocks - EARLY, tokens, width), BF16),
            pltpu.VMEM((blocks, 8, tokens), F32),
            pltpu.VMEM((padded, width), F32),
            pltpu.SemaphoreType.DMA((blocks - EARLY,)),
        ],
        compiler_params=PARAMS,
        name="attend",
    )(
        owners,
        remains,
        queries,
        pltpu.with_memory_space_constraint(early, pltpu.VMEM),
        *in_hbm(kv_cache[0]),
    )
    shares = lax.all_to_all(shares, "kv", 0, 0, tiled=True)

    everyone = ("rep", "tp")
    count = lax.axis_size("rep") * lax.axis_size("tp")
    partials = pl.pallas_call(
        merge_kernel,
        out_shape=shape((count, rows, features), BF16),
        in_specs=[VMEM] * 5,
        out_specs=VMEM,
        compiler_params=PARAMS,
        name="merge",
    )(shares, query, fresh, homed, out_weight)
    partials = lax.all_to_all(partials, everyone, 0, 0, tiled=True)

    residual, partial = pl.pallas_call(
        hidden_kernel,
        out_shape=(shape((rows, features), F32), shape((rows, features), BF16)),
        in_specs=[VMEM] * 5,
        out_specs=(VMEM,) * 2,
        compiler_params=PARAMS,
        name="hidden",
    )(token_state, partials, mlp_gain[None], up_weight.T, down_weight)
    result = pl.pallas_call(
        finish_kernel,
        out_shape=shape((rows, features), F32),
        in_specs=[VMEM] * 6,
        out_specs=VMEM,
        compiler_params=PARAMS,
        name="finish",
    )(served, residual, partial, *from_others(partial, "tp"))
    return (result[None], entries[None])


def solution(mesh):
    return jax.shard_map(
        body,
        mesh=mesh,
        in_specs=(
            P("kv", None),
            P(),
            P(None, "tp"),
            P("tp", None),
            P(),
            P(None, "tp"),
            P("tp", None),
            P("rep", "kv", None, "tp"),
            P(),
            P(),
            P(),
            P("rep", "kv"),
            P("rep", "kv"),
        ),
        out_specs=(P("rep", "kv", None), P("rep", "kv", "tp")),
        check_vma=False,
    )
```

```python
import functools

import jax
import jax.numpy as jnp
from jax import lax
from jax.experimental import pallas as pl
from jax.experimental.pallas import tpu as pltpu
from jax.sharding import PartitionSpec as P

HD = 80
PAIR = 2 * HD
VERY_LOW = -1e30
NORM_EPS = 1e-06
EARLY = 4
STATS = 320
WIDE = 384
F32 = jnp.float32
BF16 = jnp.bfloat16

VMEM = pl.BlockSpec(memory_space=pltpu.VMEM)
HBM = pl.BlockSpec(memory_space=pltpu.HBM)
SMEM = pl.BlockSpec(memory_space=pltpu.SMEM)
PARAMS = pltpu.CompilerParams(vmem_limit_bytes=16 * 1024 * 1024)


def in_hbm(*arrays):
    return [pltpu.with_memory_space_constraint(a, pltpu.HBM) for a in arrays]


def iota(shape, axis):
    return lax.broadcasted_iota(jnp.int32, shape, axis)


def root_norm(values, gain):
    mean = jnp.mean(values * values, axis=-1, keepdims=True)
    return values * lax.rsqrt(mean + NORM_EPS) * gain


def row_values(ref, start, rows, lanes):
    row = iota((rows, lanes), 0)
    out = jnp.zeros((rows, lanes), jnp.int32)
    for r in range(rows):
        out = jnp.where(row == r, ref[start + r], out)
    return out


def widen(value, lanes):
    return jnp.concatenate([value] * (lanes // value.shape[1]), axis=1)


def split3(value):
    high = value.astype(BF16).astype(F32)
    rest = value - high
    middle = rest.astype(BF16).astype(F32)
    return high, middle, (rest - middle).astype(BF16).astype(F32)


def dot_transposed(left, right):
    return lax.dot_general(left, right, (((1,), (1,)), ((), ())), preferred_element_type=F32)


def fetch(pairs, sems):
    copies = [pltpu.make_async_copy(a, b, sems.at[i]) for i, (a, b) in enumerate(pairs)]
    for copy in copies:
        copy.start()
    return copies


def query_kernel(
    token_hbm, gain_hbm, weight_hbm, spread, query, normed, token, gain, weight, sems
):
    rows = token.shape[0]
    heads = weight_hbm.shape[0] // (3 * HD)
    copies = fetch(
        [(token_hbm, token), (gain_hbm, gain.at[0])]
        + [
            (weight_hbm.at[3 * HD * h : 3 * HD * h + HD], weight.at[HD * h : HD * (h + 1)])
            for h in range(heads)
        ],
        sems,
    )
    weight[heads * HD :, :] = jnp.zeros((WIDE - heads * HD, weight.shape[1]), BF16)
    copies[0].wait()
    copies[1].wait()
    norm = root_norm(token[...].astype(F32), gain[...]).astype(BF16)
    normed[...] = norm
    for copy in copies[2:]:
        copy.wait()
    own = (dot_transposed(norm, weight[...]) * HD ** (-0.5)).astype(BF16)
    query[...] = own
    for copy in range(spread.shape[0] // rows):
        spread[copy * rows : (copy + 1) * rows, :] = own


def side_kernel(
    place,
    owner_hbm,
    index_hbm,
    length_hbm,
    home_hbm,
    moving_hbm,
    cache_hbm,
    weight_hbm,
    normed,
    cache,
    owners,
    remains,
    fresh,
    entries,
    homed,
    served,
    owner,
    index,
    length,
    home,
    moving,
    weight,
    sems,
):
    rows = normed.shape[0]
    blocks, tokens, _ = cache_hbm.shape
    heads = weight_hbm.shape[0] // (3 * HD)
    requests = length.shape[0]
    copies = fetch(
        [
            (owner_hbm, owner),
            (index_hbm, index),
            (length_hbm, length),
            (home_hbm, home),
            (moving_hbm, moving),
        ]
        + [
            (
                weight_hbm.at[3 * HD * h + HD : 3 * HD * (h + 1)],
                weight.at[PAIR * h : PAIR * (h + 1)],
            )
            for h in range(heads)
        ]
        + [(cache_hbm.at[: cache.shape[0]], cache)],
        sems,
    )
    for copy in copies[:5]:
        copy.wait()
    row = iota(owners.shape, 0)
    holders = jnp.full(owners.shape, requests, jnp.int32)
    left = jnp.zeros(owners.shape, jnp.int32)
    for b in range(blocks):
        holder = owner[0, b]
        most = jnp.where(holder < requests, length[jnp.minimum(holder, requests - 1)], 0)
        holders = jnp.where(row == b, holder, holders)
        left = jnp.where(row == b, most - index[0, b] * tokens, left)
    owners[...] = holders
    remains[...] = left
    start = place[1] * rows
    at_home = row_values(home, start, rows, 128)
    target = at_home ^ row_values(moving, start, rows, 128)
    homed[...] = jnp.where(at_home == place[0], 1.0, 0.0)
    serves = jnp.where(target == place[0], 1.0, 0.0)
    served[...] = serves
    for copy in copies[5:-1]:
        copy.wait()
    pairs = dot_transposed(normed[...], weight[...])
    fresh[...] = pairs
    entries[...] = jnp.where(widen(serves, pairs.shape[1]) > 0.0, pairs, 0.0)
    copies[-1].wait()


def attend_kernel(
    owner_of, remains, queries, early, cache_hbm, out, mark, late, scores, sums, sems
):
    blocks, tokens, width = cache_hbm.shape
    ready = early.shape[0]
    copies = fetch(
        [(cache_hbm.at[b], late.at[b - ready]) for b in range(ready, blocks)], sems
    )

    def cache(b):
        return early[b] if b < ready else late[b - ready]

    heads = width // PAIR
    requests = queries.shape[0]
    rows = sums.shape[0]
    onehot = (iota((rows, requests), 1) == widen(owner_of[...], requests)).astype(BF16)
    picked = jnp.dot(onehot, queries[...], preferred_element_type=F32)
    picked = jnp.concatenate([picked, jnp.zeros((rows, width - WIDE), F32)], axis=1)
    mark[...] = picked[:8, :128]
    lane = iota((rows, width), 1)
    spread = jnp.zeros((rows, width), F32)
    for h in range(heads):
        moved = picked if h == 0 else pltpu.roll(picked, HD * h, 1)
        spread = jnp.where((lane >= PAIR * h) & (lane < PAIR * h + HD), moved, spread)
    head_lane = iota((8, width), 1) - PAIR * iota((8, width), 0)
    key_lanes = (head_lane >= 0) & (head_lane < HD)
    value_lanes = (head_lane >= HD) & (head_lane < PAIR)
    block_lane = iota((8, 128), 1)
    token_lane = iota((8, tokens), 1)
    every_peak = jnp.full((8, 128), VERY_LOW, F32)
    holders = jnp.full((8, 128), requests, jnp.int32)
    usable = []
    for b in range(blocks):
        ask = jnp.where(key_lanes, jnp.broadcast_to(spread[b : b + 1], (8, width)), 0.0)
        if b >= ready:
            copies[b - ready].wait()
        score = dot_transposed(ask.astype(BF16), cache(b))
        use = token_lane < widen(jnp.broadcast_to(remains[b : b + 1, :], (8, 128)), tokens)
        score = jnp.where(use, score, VERY_LOW)
        scores[b] = score
        usable.append(use)
        peak = jnp.max(score, axis=1, keepdims=True)
        every_peak = jnp.where(block_lane == b, peak, every_peak)
        holders = jnp.where(block_lane == b, owner_of[b : b + 1, :], holders)
    stat_lane = iota((8, 128), 1) - (STATS - 256)
    stat_row = iota((8, 128), 0)
    stats = []
    for b in range(blocks):
        peers = jnp.where(holders == owner_of[b : b + 1, :], every_peak, VERY_LOW)
        joint = jnp.max(peers, axis=1, keepdims=True)
        weights = jnp.where(usable[b], jnp.exp(scores[b] - joint), 0.0)
        total = jnp.sum(weights, axis=1, keepdims=True)
        acc = jnp.dot(weights.astype(BF16), cache(b), preferred_element_type=F32)
        sums[b : b + 1, :] = jnp.sum(jnp.where(value_lanes, acc, 0.0), axis=0, keepdims=True)
        stat = jnp.where(stat_lane == stat_row, joint, 0.0)
        stat = stat + jnp.where(stat_lane == stat_row + 8, total, 0.0)
        stats.append(jnp.sum(jnp.where(stat_row < heads, stat, 0.0), axis=0, keepdims=True))
    stats += [jnp.zeros((1, 128), F32)] * (rows - blocks)
    stats = jnp.concatenate(stats, axis=0)
    sums[blocks:rows, :] = jnp.zeros((rows - blocks, width), F32)
    packed = jnp.zeros((rows, width), F32)
    every = sums[...]
    for h in range(heads):
        moved = pltpu.roll(every, width - HD * (h + 1), 1)
        packed = jnp.where((lane >= HD * h) & (lane < HD * (h + 1)), moved, packed)
    packed = packed[:, :WIDE]
    added = jnp.zeros((rows, WIDE), F32)
    totals = jnp.zeros((rows, 128), F32)
    first = iota((rows, 128), 0) < blocks
    for b in range(blocks):
        same = owner_of[...] == owner_of[b : b + 1, :]
        added = added + jnp.where(widen(same, WIDE), packed[b : b + 1], 0.0)
        totals = totals + jnp.where(same, stats[b : b + 1], 0.0)
        first = first & ((iota((rows, 128), 0) <= b) | ~same)
    tail = iota((rows, 128), 1) - (STATS - 256)
    peak_part = jnp.where((tail >= 0) & (tail < 8), stats, 0.0)
    total_part = jnp.where((tail >= 8) & (tail < 16), totals, 0.0)
    parts = jnp.zeros((rows, 128), F32)
    for k, part in enumerate(split3(peak_part)):
        parts = parts + (part if k == 0 else pltpu.roll(part, 16 * k, 1))
    for k, part in enumerate(split3(total_part)):
        parts = parts + (part if k == 0 else pltpu.roll(part, 16 * k, 1))
    last = jnp.where(tail >= 0, parts, added[:, 256:])
    full = jnp.concatenate([added[:, :256], last], axis=1)
    keep = jnp.where(first, 1.0, 0.0)
    full = jnp.where(widen(keep, WIDE) > 0.0, full, 0.0).astype(BF16)
    out[...] = lax.dot_general(
        onehot,
        full,
        (((0,), (0,)), ((), ())),
        preferred_element_type=F32,
    ).astype(BF16)


def self_kernel(
    mark,
    query,
    fresh,
    token_hbm,
    gain_hbm,
    out_hbm,
    up_hbm,
    down_hbm,
    scores,
    values,
    token,
    gain,
    out,
    up,
    down,
    sems,
):
    copies = fetch(
        [
            (token_hbm, token),
            (gain_hbm, gain.at[0]),
            (out_hbm, out),
            (up_hbm, up),
            (down_hbm, down),
        ],
        sems,
    )
    rows, width = fresh.shape
    heads = width // PAIR
    pair = fresh[...].astype(BF16).astype(F32)
    own = query[...].astype(F32)
    keys = jnp.concatenate([pair[:, PAIR * h : PAIR * h + HD] for h in range(heads)], axis=1)
    values[...] = jnp.concatenate(
        [pair[:, PAIR * h + HD : PAIR * (h + 1)] for h in range(heads)]
        + [jnp.zeros((rows, WIDE - heads * HD), F32)],
        axis=1,
    )
    product = own[:, : heads * HD] * keys
    head_of = iota((rows, heads * HD), 1) // HD
    own_lane = iota((rows, 128), 1) - (STATS - 256)
    self_score = jnp.full((rows, 128), VERY_LOW, F32)
    for h in range(heads):
        score = jnp.sum(jnp.where(head_of == h, product, 0.0), axis=1, keepdims=True)
        self_score = jnp.where(own_lane == h, score, self_score)
    scores[...] = self_score
    for copy in copies:
        copy.wait()


def merge_kernel(shares, self_scores, values, homed, weight, spread):
    rows = values.shape[0]
    count = shares.shape[0] // rows
    heads = weight.shape[0] // HD
    sums = shares[...].astype(F32)
    tail = sums[:, 256:]
    joined = tail + pltpu.roll(tail, 128 - 16, 1) + pltpu.roll(tail, 128 - 32, 1)
    totals = pltpu.roll(joined, 128 - 8, 1)
    lane = iota(joined.shape, 1) - (STATS - 256)
    peaks = jnp.where((lane >= 0) & (lane < heads) & (totals > 0.0), joined, VERY_LOW)
    self_score = self_scores[...]
    top = self_score
    for s in range(count):
        top = jnp.maximum(top, peaks[s * rows : (s + 1) * rows])
    denominator = jnp.exp(self_score - top)
    self_weight = denominator.astype(BF16).astype(F32)
    wide_of = iota((rows, WIDE), 1) // HD

    def per_head(value):
        out = jnp.zeros((rows, WIDE), F32)
        for h in range(heads):
            at = STATS - 256 + h
            out = jnp.where(wide_of == h, value[:, at : at + 1], out)
        return out

    numerator = per_head(self_weight) * values[...]
    for s in range(count):
        at = slice(s * rows, (s + 1) * rows)
        factor = jnp.exp(peaks[at] - top)
        denominator = denominator + factor * totals[at]
        numerator = numerator + per_head(factor) * sums[at]
    result = numerator / jnp.where(wide_of < heads, per_head(denominator), 1.0)
    attended = jnp.where(widen(homed[...], WIDE) > 0.0, result, 0.0).astype(BF16)
    partial = jnp.dot(
        attended[:, : weight.shape[0]], weight[...], preferred_element_type=F32
    ).astype(BF16)
    for copy in range(spread.shape[0]):
        spread[copy] = partial


def hidden_kernel(token, shares, gain, up, down, residual, partial):
    total = token[...].astype(F32)
    for share in range(shares.shape[0]):
        total = total + shares[share].astype(F32)
    residual[...] = total
    normed = root_norm(total, gain[...]).astype(BF16)
    hidden = dot_transposed(normed, up[...])
    active = jax.nn.gelu(hidden, approximate=True).astype(BF16)
    partial[...] = jnp.dot(active, down[...], preferred_element_type=F32).astype(BF16)


def finish_kernel(served, residual, own, across, near, far, out):
    own, across, near, far = (v[...].astype(F32) for v in (own, across, near, far))
    result = residual[...] + ((own + across) + (near + far))
    out[...] = jnp.where(widen(served[...], result.shape[1]) > 0.0, result, 0.0)


def shape(dims, dtype):
    return jax.ShapeDtypeStruct(dims, dtype)


def exchanged(value, partner):
    axes = ("rep", "tp")
    count = lax.axis_size("rep") * lax.axis_size("tp")
    return lax.ppermute(value, axes, [(i, partner(i) % count) for i in range(count)])


def from_others(value):
    return (
        exchanged(value, lambda i: i ^ 2),
        exchanged(value, lambda i: i ^ 1),
        exchanged(value, lambda i: i + 1 if i % 2 else i - 1),
    )


def body(
    token_state,
    attn_gain,
    qkv_weight,
    out_weight,
    mlp_gain,
    up_weight,
    down_weight,
    kv_cache,
    home_replica,
    moving,
    cache_length,
    block_owner,
    block_index,
):
    rows, features = token_state.shape
    requests = home_replica.shape[0]
    _, blocks, tokens, width = kv_cache.shape
    heads = width // PAIR
    place = jnp.stack([lax.axis_index("rep"), lax.axis_index("kv")]).astype(jnp.int32)

    weight = qkv_weight.T
    spread, query, normed = pl.pallas_call(
        query_kernel,
        out_shape=(
            shape((requests, WIDE), BF16),
            shape((rows, WIDE), BF16),
            shape((rows, features), BF16),
        ),
        in_specs=[HBM] * 3,
        out_specs=(VMEM,) * 3,
        scratch_shapes=[
            pltpu.VMEM((rows, features), BF16),
            pltpu.VMEM((1, features), F32),
            pltpu.VMEM((WIDE, features), BF16),
            pltpu.SemaphoreType.DMA((2 + heads,)),
        ],
        compiler_params=PARAMS,
        name="query",
    )(*in_hbm(token_state, attn_gain, weight))
    queries = lax.all_to_all(spread, "kv", 0, 0, tiled=True)

    padded = -(-blocks // 16) * 16
    early, owners, remains, fresh, entries, homed, served = pl.pallas_call(
        side_kernel,
        out_shape=(
            pltpu.VMEM((EARLY, tokens, width), BF16),
            shape((padded, 128), jnp.int32),
            shape((padded, 128), jnp.int32),
            shape((rows, width), F32),
            shape((rows, width), F32),
            shape((rows, 128), F32),
            shape((rows, 128), F32),
        ),
        in_specs=[SMEM] + [HBM] * 7 + [VMEM],
        out_specs=(VMEM,) * 7,
        scratch_shapes=[pltpu.SMEM((1, blocks), jnp.int32)] * 2
        + [pltpu.SMEM((requests,), jnp.int32)] * 3
        + [pltpu.VMEM((width, features), BF16), pltpu.SemaphoreType.DMA((6 + heads,))],
        compiler_params=PARAMS,
        cost_estimate=pl.CostEstimate(
            flops=0, bytes_accessed=2 * EARLY * tokens * width * 2, transcendentals=0
        ),
        name="side",
    )(
        place,
        *in_hbm(
            block_owner, block_index, cache_length, home_replica, moving, kv_cache[0], weight
        ),
        normed,
    )

    shares, mark = pl.pallas_call(
        attend_kernel,
        out_shape=(shape((requests, WIDE), BF16), shape((8, 128), F32)),
        in_specs=[VMEM] * 4 + [HBM],
        out_specs=(VMEM,) * 2,
        scratch_shapes=[
            pltpu.VMEM((blocks - EARLY, tokens, width), BF16),
            pltpu.VMEM((blocks, 8, tokens), F32),
            pltpu.VMEM((padded, width), F32),
            pltpu.SemaphoreType.DMA((blocks - EARLY,)),
        ],
        compiler_params=PARAMS,
        name="attend",
    )(
        owners,
        remains,
        queries,
        pltpu.with_memory_space_constraint(early, pltpu.VMEM),
        *in_hbm(kv_cache[0]),
    )
    shares = lax.all_to_all(shares, "kv", 0, 0, tiled=True)

    later = (out_weight, up_weight.T, down_weight)
    held = [pltpu.VMEM((rows, features), BF16), pltpu.VMEM((1, features), F32)]
    held += [pltpu.VMEM(w.shape, BF16) for w in later]
    self_scores, values, *kept = pl.pallas_call(
        self_kernel,
        out_shape=(shape((rows, 128), F32), shape((rows, WIDE), F32), *held),
        in_specs=[VMEM] * 3 + [HBM] * 5,
        out_specs=(VMEM,) * 7,
        scratch_shapes=[pltpu.SemaphoreType.DMA((5,))],
        compiler_params=PARAMS,
        cost_estimate=pl.CostEstimate(
            flops=0, bytes_accessed=2 * sum(w.size for w in later) * 2, transcendentals=0
        ),
        name="self",
    )(mark, query, fresh, *in_hbm(token_state, mlp_gain, *later))
    token, gain, out_kept, up_kept, down_kept = (
        pltpu.with_memory_space_constraint(k, pltpu.VMEM) for k in kept
    )

    everyone = ("rep", "tp")
    count = lax.axis_size("rep") * lax.axis_size("tp")
    partials = pl.pallas_call(
        merge_kernel,
        out_shape=shape((count, rows, features), BF16),
        in_specs=[VMEM] * 5,
        out_specs=VMEM,
        compiler_params=PARAMS,
        name="merge",
    )(shares, self_scores, values, homed, out_kept)
    partials = lax.all_to_all(partials, everyone, 0, 0, tiled=True)

    residual, partial = pl.pallas_call(
        hidden_kernel,
        out_shape=(shape((rows, features), F32), shape((rows, features), BF16)),
        in_specs=[VMEM] * 5,
        out_specs=(VMEM,) * 2,
        compiler_params=PARAMS,
        name="hidden",
    )(token, partials, gain, up_kept, down_kept)
    result = pl.pallas_call(
        finish_kernel,
        out_shape=shape((rows, features), F32),
        in_specs=[VMEM] * 6,
        out_specs=VMEM,
        compiler_params=PARAMS,
        name="finish",
    )(served, residual, partial, *from_others(partial))
    return (result[None], entries[None])


def solution(mesh):
    return jax.shard_map(
        body,
        mesh=mesh,
        in_specs=(
            P("kv", None),
            P(),
            P(None, "tp"),
            P("tp", None),
            P(),
            P(None, "tp"),
            P("tp", None),
            P("rep", "kv", None, "tp"),
            P(),
            P(),
            P(),
            P("rep", "kv"),
            P("rep", "kv"),
        ),
        out_specs=(P("rep", "kv", None), P("rep", "kv", "tp")),
        check_vma=False,
    )
```

```python
import functools

import jax
import jax.numpy as jnp
from jax import lax
from jax.experimental import pallas as pl
from jax.experimental.pallas import tpu as pltpu
from jax.sharding import PartitionSpec as P

HD = 80
PAIR = 2 * HD
VERY_LOW = -1e30
NORM_EPS = 1e-06
EARLY = 3
LATE_GROUP = 2
STATS = 320
WIDE = 384
F32 = jnp.float32
BF16 = jnp.bfloat16

VMEM = pl.BlockSpec(memory_space=pltpu.VMEM)
HBM = pl.BlockSpec(memory_space=pltpu.HBM)
SMEM = pl.BlockSpec(memory_space=pltpu.SMEM)
PARAMS = pltpu.CompilerParams(vmem_limit_bytes=16 * 1024 * 1024)


def in_hbm(*arrays):
    return [pltpu.with_memory_space_constraint(a, pltpu.HBM) for a in arrays]


def iota(shape, axis):
    return lax.broadcasted_iota(jnp.int32, shape, axis)


def root_norm(values, gain):
    mean = jnp.mean(values * values, axis=-1, keepdims=True)
    return values * lax.rsqrt(mean + NORM_EPS) * gain


def row_values(ref, start, rows, lanes):
    row = iota((rows, lanes), 0)
    out = jnp.zeros((rows, lanes), jnp.int32)
    for r in range(rows):
        out = jnp.where(row == r, ref[start + r], out)
    return out


def widen(value, lanes):
    return jnp.concatenate([value] * (lanes // value.shape[1]), axis=1)


def split3(value):
    high = value.astype(BF16).astype(F32)
    rest = value - high
    middle = rest.astype(BF16).astype(F32)
    return high, middle, (rest - middle).astype(BF16).astype(F32)


def dot_transposed(left, right):
    return lax.dot_general(left, right, (((1,), (1,)), ((), ())), preferred_element_type=F32)


def fetch(pairs, sems):
    copies = [pltpu.make_async_copy(a, b, sems.at[i]) for i, (a, b) in enumerate(pairs)]
    for copy in copies:
        copy.start()
    return copies


def query_kernel(
    token_hbm, gain_hbm, weight_hbm, spread, query, normed, token, gain, weight, sems
):
    rows = token.shape[0]
    heads = weight_hbm.shape[0] // (3 * HD)
    copies = fetch(
        [(token_hbm, token), (gain_hbm, gain.at[0])]
        + [
            (weight_hbm.at[3 * HD * h : 3 * HD * h + HD], weight.at[HD * h : HD * (h + 1)])
            for h in range(heads)
        ],
        sems,
    )
    weight[heads * HD :, :] = jnp.zeros((WIDE - heads * HD, weight.shape[1]), BF16)
    copies[0].wait()
    copies[1].wait()
    norm = root_norm(token[...].astype(F32), gain[...]).astype(BF16)
    normed[...] = norm
    for copy in copies[2:]:
        copy.wait()
    own = (dot_transposed(norm, weight[...]) * HD ** (-0.5)).astype(BF16)
    query[...] = own
    for copy in range(spread.shape[0] // rows):
        spread[copy * rows : (copy + 1) * rows, :] = own


def side_kernel(
    place,
    owner_hbm,
    index_hbm,
    length_hbm,
    home_hbm,
    moving_hbm,
    cache_hbm,
    weight_hbm,
    gain_hbm,
    normed,
    query,
    cache,
    owners,
    remains,
    entries,
    homed,
    served,
    self_scores,
    values,
    gain,
    owner,
    index,
    length,
    home,
    moving,
    weight,
    sems,
):
    rows = normed.shape[0]
    blocks, tokens, _ = cache_hbm.shape
    heads = weight_hbm.shape[0] // (3 * HD)
    requests = length.shape[0]
    copies = fetch(
        [
            (owner_hbm, owner),
            (index_hbm, index),
            (length_hbm, length),
            (home_hbm, home),
            (moving_hbm, moving),
        ]
        + [
            (
                weight_hbm.at[3 * HD * h + HD : 3 * HD * (h + 1)],
                weight.at[PAIR * h : PAIR * (h + 1)],
            )
            for h in range(heads)
        ]
        + [(gain_hbm, gain.at[0]), (cache_hbm.at[: cache.shape[0]], cache)],
        sems,
    )
    for copy in copies[:5]:
        copy.wait()
    row = iota(owners.shape, 0)
    holders = jnp.full(owners.shape, requests, jnp.int32)
    left = jnp.zeros(owners.shape, jnp.int32)
    for b in range(blocks):
        holder = owner[0, b]
        most = jnp.where(holder < requests, length[jnp.minimum(holder, requests - 1)], 0)
        holders = jnp.where(row == b, holder, holders)
        left = jnp.where(row == b, most - index[0, b] * tokens, left)
    owners[...] = holders
    remains[...] = left
    start = place[1] * rows
    at_home = row_values(home, start, rows, 128)
    target = at_home ^ row_values(moving, start, rows, 128)
    homed[...] = jnp.where(at_home == place[0], 1.0, 0.0)
    serves = jnp.where(target == place[0], 1.0, 0.0)
    served[...] = serves
    for copy in copies[5:-1]:
        copy.wait()
    pairs = dot_transposed(normed[...], weight[...])
    entries[...] = jnp.where(widen(serves, pairs.shape[1]) > 0.0, pairs, 0.0)
    pair = pairs.astype(BF16).astype(F32)
    keys = jnp.concatenate([pair[:, PAIR * h : PAIR * h + HD] for h in range(heads)], axis=1)
    values[...] = jnp.concatenate(
        [pair[:, PAIR * h + HD : PAIR * (h + 1)] for h in range(heads)]
        + [jnp.zeros((rows, WIDE - heads * HD), F32)],
        axis=1,
    )
    product = query[...].astype(F32)[:, : heads * HD] * keys
    head_of = iota((rows, heads * HD), 1) // HD
    own_lane = iota((rows, 128), 1) - (STATS - 256)
    self_score = jnp.full((rows, 128), VERY_LOW, F32)
    for h in range(heads):
        score = jnp.sum(jnp.where(head_of == h, product, 0.0), axis=1, keepdims=True)
        self_score = jnp.where(own_lane == h, score, self_score)
    self_scores[...] = self_score
    copies[-1].wait()


def attend_kernel(
    owner_of, remains, queries, early, cache_hbm, out, late, parts, sums, sems
):
    blocks, tokens, width = cache_hbm.shape
    ready = early.shape[0]
    copies = fetch(
        [(cache_hbm.at[b], late.at[b - ready]) for b in range(ready, blocks)], sems
    )

    def cache(b):
        return early[b] if b < ready else late[b - ready]

    heads = width // PAIR
    requests = queries.shape[0]
    rows = sums.shape[0]
    onehot = (iota((rows, requests), 1) == widen(owner_of[...], requests)).astype(BF16)
    picked = jnp.dot(onehot, queries[...], preferred_element_type=F32)
    picked = jnp.concatenate([picked, jnp.zeros((rows, width - WIDE), F32)], axis=1)
    lane = iota((rows, width), 1)
    spread = jnp.zeros((rows, width), F32)
    for h in range(heads):
        moved = picked if h == 0 else pltpu.roll(picked, HD * h, 1)
        spread = jnp.where((lane >= PAIR * h) & (lane < PAIR * h + HD), moved, spread)
    head_lane = iota((8, width), 1) - PAIR * iota((8, width), 0)
    key_lanes = (head_lane >= 0) & (head_lane < HD)
    value_lanes = (head_lane >= HD) & (head_lane < PAIR)
    block_lane = iota((8, 128), 1)
    token_lane = iota((8, tokens), 1)
    every_peak = jnp.full((8, 128), VERY_LOW, F32)
    holders = jnp.full((8, 128), requests, jnp.int32)
    scores = [None] * blocks
    uses = [None] * blocks
    peaks = [None] * blocks
    totals = [None] * blocks

    def weigh(group):
        for b in group:
            peaks[b] = jnp.max(scores[b], axis=1, keepdims=True)
        for b in group:
            weights = jnp.where(uses[b], jnp.exp(scores[b] - peaks[b]), 0.0)
            totals[b] = jnp.sum(weights, axis=1, keepdims=True)
            acc = jnp.dot(weights.astype(BF16), cache(b), preferred_element_type=F32)
            parts[b] = jnp.where(value_lanes, acc, 0.0)

    before = ()
    starts = [0] + list(range(ready, blocks, LATE_GROUP)) + [blocks]
    for g in range(len(starts) - 1):
        group = range(starts[g], starts[g + 1])
        for b in group:
            if b >= ready:
                copies[b - ready].wait()
        for b in group:
            ask = jnp.where(key_lanes, jnp.broadcast_to(spread[b : b + 1], (8, width)), 0.0)
            score = dot_transposed(ask.astype(BF16), cache(b))
            left = widen(jnp.broadcast_to(remains[b : b + 1, :], (8, 128)), tokens)
            uses[b] = token_lane < left
            scores[b] = jnp.where(uses[b], score, VERY_LOW)
        weigh(before)
        before = group
    weigh(before)
    for b in range(blocks):
        every_peak = jnp.where(block_lane == b, peaks[b], every_peak)
        holders = jnp.where(block_lane == b, owner_of[b : b + 1, :], holders)
    stat_lane = iota((8, 128), 1) - (STATS - 256)
    stat_row = iota((8, 128), 0)
    stats = []
    for b in range(blocks):
        peers = jnp.where(holders == owner_of[b : b + 1, :], every_peak, VERY_LOW)
        joint = jnp.max(peers, axis=1, keepdims=True)
        factor = jnp.exp(peaks[b] - joint)
        sums[b : b + 1, :] = jnp.sum(parts[b] * factor, axis=0, keepdims=True)
        stat = jnp.where(stat_lane == stat_row, joint, 0.0)
        stat = stat + jnp.where(stat_lane == stat_row + 8, totals[b] * factor, 0.0)
        stats.append(jnp.sum(jnp.where(stat_row < heads, stat, 0.0), axis=0, keepdims=True))
    stats += [jnp.zeros((1, 128), F32)] * (rows - blocks)
    stats = jnp.concatenate(stats, axis=0)
    sums[blocks:rows, :] = jnp.zeros((rows - blocks, width), F32)
    packed = jnp.zeros((rows, width), F32)
    every = sums[...]
    for h in range(heads):
        moved = pltpu.roll(every, width - HD * (h + 1), 1)
        packed = jnp.where((lane >= HD * h) & (lane < HD * (h + 1)), moved, packed)
    packed = packed[:, :WIDE]
    added = jnp.zeros((rows, WIDE), F32)
    added_totals = jnp.zeros((rows, 128), F32)
    first = iota((rows, 128), 0) < blocks
    for b in range(blocks):
        same = owner_of[...] == owner_of[b : b + 1, :]
        added = added + jnp.where(widen(same, WIDE), packed[b : b + 1], 0.0)
        added_totals = added_totals + jnp.where(same, stats[b : b + 1], 0.0)
        first = first & ((iota((rows, 128), 0) <= b) | ~same)
    tail = iota((rows, 128), 1) - (STATS - 256)
    peak_part = jnp.where((tail >= 0) & (tail < 8), stats, 0.0)
    total_part = jnp.where((tail >= 8) & (tail < 16), added_totals, 0.0)
    terms = jnp.zeros((rows, 128), F32)
    for k, term in enumerate(split3(peak_part + total_part)):
        terms = terms + (term if k == 0 else pltpu.roll(term, 16 * k, 1))
    last = jnp.where(tail >= 0, terms, added[:, 256:])
    full = jnp.concatenate([added[:, :256], last], axis=1)
    keep = jnp.where(first, 1.0, 0.0)
    full = jnp.where(widen(keep, WIDE) > 0.0, full, 0.0).astype(BF16)
    out[...] = lax.dot_general(
        onehot,
        full,
        (((0,), (0,)), ((), ())),
        preferred_element_type=F32,
    ).astype(BF16)


def merge_kernel(shares, self_scores, values, homed, weight, spread):
    rows = values.shape[0]
    count = shares.shape[0] // rows
    heads = weight.shape[0] // HD
    sums = shares[...].astype(F32)
    tail = sums[:, 256:]
    joined = tail + pltpu.roll(tail, 128 - 16, 1) + pltpu.roll(tail, 128 - 32, 1)
    totals = pltpu.roll(joined, 128 - 8, 1)
    lane = iota(joined.shape, 1) - (STATS - 256)
    peaks = jnp.where((lane >= 0) & (lane < heads) & (totals > 0.0), joined, VERY_LOW)
    self_score = self_scores[...]
    top = self_score
    for s in range(count):
        top = jnp.maximum(top, peaks[s * rows : (s + 1) * rows])
    denominator = jnp.exp(self_score - top)
    self_weight = denominator.astype(BF16).astype(F32)
    wide_of = iota((rows, WIDE), 1) // HD

    def per_head(value):
        out = jnp.zeros((rows, WIDE), F32)
        for h in range(heads):
            at = STATS - 256 + h
            out = jnp.where(wide_of == h, value[:, at : at + 1], out)
        return out

    numerator = per_head(self_weight) * values[...]
    for s in range(count):
        at = slice(s * rows, (s + 1) * rows)
        factor = jnp.exp(peaks[at] - top)
        denominator = denominator + factor * totals[at]
        numerator = numerator + per_head(factor) * sums[at]
    result = numerator / jnp.where(wide_of < heads, per_head(denominator), 1.0)
    attended = jnp.where(widen(homed[...], WIDE) > 0.0, result, 0.0).astype(BF16)
    partial = jnp.dot(
        attended[:, : weight.shape[0]], weight[...], preferred_element_type=F32
    ).astype(BF16)
    for copy in range(spread.shape[0]):
        spread[copy] = partial


def hidden_kernel(token, shares, gain, up, down, residual, partial):
    total = token[...].astype(F32)
    for share in range(shares.shape[0]):
        total = total + shares[share].astype(F32)
    residual[...] = total
    normed = root_norm(total, gain[...]).astype(BF16)
    hidden = dot_transposed(normed, up[...])
    active = jax.nn.gelu(hidden, approximate=True).astype(BF16)
    partial[...] = jnp.dot(active, down[...], preferred_element_type=F32).astype(BF16)


def finish_kernel(served, residual, own, far, near, across, out):
    own, far, near, across = (v[...].astype(F32) for v in (own, far, near, across))
    result = residual[...] + ((own + across) + (near + far))
    out[...] = jnp.where(widen(served[...], result.shape[1]) > 0.0, result, 0.0)


def shape(dims, dtype):
    return jax.ShapeDtypeStruct(dims, dtype)


def exchanged(value, partner):
    axes = ("rep", "tp")
    count = lax.axis_size("rep") * lax.axis_size("tp")
    return lax.ppermute(value, axes, [(i, partner(i) % count) for i in range(count)])


def from_others(value):
    far = exchanged(value, lambda i: i + 1 if i % 2 else i - 1)
    near = exchanged(value, lambda i: i ^ 1)
    across = exchanged(value, lambda i: i ^ 2)
    return far, near, across


def body(
    token_state,
    attn_gain,
    qkv_weight,
    out_weight,
    mlp_gain,
    up_weight,
    down_weight,
    kv_cache,
    home_replica,
    moving,
    cache_length,
    block_owner,
    block_index,
):
    rows, features = token_state.shape
    requests = home_replica.shape[0]
    _, blocks, tokens, width = kv_cache.shape
    heads = width // PAIR
    place = jnp.stack([lax.axis_index("rep"), lax.axis_index("kv")]).astype(jnp.int32)

    weight = qkv_weight.T
    spread, query, normed = pl.pallas_call(
        query_kernel,
        out_shape=(
            shape((requests, WIDE), BF16),
            shape((rows, WIDE), BF16),
            shape((rows, features), BF16),
        ),
        in_specs=[HBM] * 3,
        out_specs=(VMEM,) * 3,
        scratch_shapes=[
            pltpu.VMEM((rows, features), BF16),
            pltpu.VMEM((1, features), F32),
            pltpu.VMEM((WIDE, features), BF16),
            pltpu.SemaphoreType.DMA((2 + heads,)),
        ],
        compiler_params=PARAMS,
        name="query",
    )(*in_hbm(token_state, attn_gain, weight))
    queries = lax.all_to_all(spread, "kv", 0, 0, tiled=True)

    padded = -(-blocks // 16) * 16
    early, owners, remains, entries, homed, served, self_scores, values, gain = pl.pallas_call(
        side_kernel,
        out_shape=(
            pltpu.VMEM((EARLY, tokens, width), BF16),
            shape((padded, 128), jnp.int32),
            shape((padded, 128), jnp.int32),
            shape((rows, width), F32),
            shape((rows, 128), F32),
            shape((rows, 128), F32),
            shape((rows, 128), F32),
            shape((rows, WIDE), F32),
            shape((1, features), F32),
        ),
        in_specs=[SMEM] + [HBM] * 8 + [VMEM] * 2,
        out_specs=(VMEM,) * 9,
        scratch_shapes=[pltpu.SMEM((1, blocks), jnp.int32)] * 2
        + [pltpu.SMEM((requests,), jnp.int32)] * 3
        + [pltpu.VMEM((width, features), BF16), pltpu.SemaphoreType.DMA((7 + heads,))],
        compiler_params=PARAMS,
        cost_estimate=pl.CostEstimate(
            flops=0, bytes_accessed=2 * EARLY * tokens * width * 2, transcendentals=0
        ),
        name="side",
    )(
        place,
        *in_hbm(
            block_owner,
            block_index,
            cache_length,
            home_replica,
            moving,
            kv_cache[0],
            weight,
            mlp_gain,
        ),
        normed,
        query,
    )

    shares = pl.pallas_call(
        attend_kernel,
        out_shape=shape((requests, WIDE), BF16),
        in_specs=[VMEM] * 4 + [HBM],
        out_specs=VMEM,
        scratch_shapes=[
            pltpu.VMEM((blocks - EARLY, tokens, width), BF16),
            pltpu.VMEM((blocks, 8, width), F32),
            pltpu.VMEM((padded, width), F32),
            pltpu.SemaphoreType.DMA((blocks - EARLY,)),
        ],
        compiler_params=PARAMS,
        name="attend",
    )(
        owners,
        remains,
        queries,
        pltpu.with_memory_space_constraint(early, pltpu.VMEM),
        *in_hbm(kv_cache[0]),
    )
    shares = lax.all_to_all(shares, "kv", 0, 0, tiled=True)

    everyone = ("rep", "tp")
    count = lax.axis_size("rep") * lax.axis_size("tp")
    partials = pl.pallas_call(
        merge_kernel,
        out_shape=shape((count, rows, features), BF16),
        in_specs=[VMEM] * 5,
        out_specs=VMEM,
        compiler_params=PARAMS,
        name="merge",
    )(shares, self_scores, values, homed, out_weight)
    partials = lax.all_to_all(partials, everyone, 0, 0, tiled=True)

    residual, partial = pl.pallas_call(
        hidden_kernel,
        out_shape=(shape((rows, features), F32), shape((rows, features), BF16)),
        in_specs=[VMEM] * 5,
        out_specs=(VMEM,) * 2,
        compiler_params=PARAMS,
        name="hidden",
    )(token_state, partials, gain, up_weight.T, down_weight)
    result = pl.pallas_call(
        finish_kernel,
        out_shape=shape((rows, features), F32),
        in_specs=[VMEM] * 6,
        out_specs=VMEM,
        compiler_params=PARAMS,
        name="finish",
    )(served, residual, partial, *from_others(partial))
    return (result[None], entries[None])


def solution(mesh):
    return jax.shard_map(
        body,
        mesh=mesh,
        in_specs=(
            P("kv", None),
            P(),
            P(None, "tp"),
            P("tp", None),
            P(),
            P(None, "tp"),
            P("tp", None),
            P("rep", "kv", None, "tp"),
            P(),
            P(),
            P(),
            P("rep", "kv"),
            P("rep", "kv"),
        ),
        out_specs=(P("rep", "kv", None), P("rep", "kv", "tp")),
        check_vma=False,
    )
```

```python
import functools

import jax
import jax.numpy as jnp
from jax import lax
from jax.experimental import pallas as pl
from jax.experimental.pallas import tpu as pltpu
from jax.sharding import PartitionSpec as P

HD = 80
PAIR = 2 * HD
VERY_LOW = -1e30
NORM_EPS = 1e-06
EARLY = 3
LATE_GROUP = 2
STATS = 320
WIDE = 384
F32 = jnp.float32
BF16 = jnp.bfloat16

VMEM = pl.BlockSpec(memory_space=pltpu.VMEM)
HBM = pl.BlockSpec(memory_space=pltpu.HBM)
SMEM = pl.BlockSpec(memory_space=pltpu.SMEM)
PARAMS = pltpu.CompilerParams(vmem_limit_bytes=16 * 1024 * 1024)


def in_hbm(*arrays):
    return [pltpu.with_memory_space_constraint(a, pltpu.HBM) for a in arrays]


def iota(shape, axis):
    return lax.broadcasted_iota(jnp.int32, shape, axis)


def root_norm(values, gain):
    mean = jnp.mean(values * values, axis=-1, keepdims=True)
    return values * lax.rsqrt(mean + NORM_EPS) * gain


def row_values(ref, start, rows, lanes):
    row = iota((rows, lanes), 0)
    out = jnp.zeros((rows, lanes), jnp.int32)
    for r in range(rows):
        out = jnp.where(row == r, ref[start + r], out)
    return out


def widen(value, lanes):
    return jnp.concatenate([value] * (lanes // value.shape[1]), axis=1)


def split3(value):
    high = value.astype(BF16).astype(F32)
    rest = value - high
    middle = rest.astype(BF16).astype(F32)
    return high, middle, (rest - middle).astype(BF16).astype(F32)


def dot_transposed(left, right):
    return lax.dot_general(left, right, (((1,), (1,)), ((), ())), preferred_element_type=F32)


def fetch(pairs, sems):
    copies = [pltpu.make_async_copy(a, b, sems.at[i]) for i, (a, b) in enumerate(pairs)]
    for copy in copies:
        copy.start()
    return copies


def query_kernel(
    token_hbm, gain_hbm, weight_hbm, spread, query, normed, token, gain, weight, sems
):
    rows = token.shape[0]
    heads = weight_hbm.shape[0] // (3 * HD)
    copies = fetch(
        [(token_hbm, token), (gain_hbm, gain.at[0])]
        + [
            (weight_hbm.at[3 * HD * h : 3 * HD * h + HD], weight.at[HD * h : HD * (h + 1)])
            for h in range(heads)
        ],
        sems,
    )
    weight[heads * HD :, :] = jnp.zeros((WIDE - heads * HD, weight.shape[1]), BF16)
    copies[0].wait()
    copies[1].wait()
    norm = root_norm(token[...].astype(F32), gain[...]).astype(BF16)
    normed[...] = norm
    for copy in copies[2:]:
        copy.wait()
    own = (dot_transposed(norm, weight[...]) * HD ** (-0.5)).astype(BF16)
    query[...] = own
    for copy in range(spread.shape[0] // rows):
        spread[copy * rows : (copy + 1) * rows, :] = own


def side_kernel(
    place,
    owner_hbm,
    index_hbm,
    length_hbm,
    home_hbm,
    moving_hbm,
    cache_hbm,
    weight_hbm,
    gain_hbm,
    normed,
    query,
    cache,
    owners,
    remains,
    entries,
    homed,
    served,
    self_scores,
    values,
    gain,
    owner,
    index,
    length,
    home,
    moving,
    weight,
    sems,
):
    rows = normed.shape[0]
    blocks, tokens, _ = cache_hbm.shape
    heads = weight_hbm.shape[0] // (3 * HD)
    requests = length.shape[0]
    copies = fetch(
        [
            (owner_hbm, owner),
            (index_hbm, index),
            (length_hbm, length),
            (home_hbm, home),
            (moving_hbm, moving),
        ]
        + [
            (
                weight_hbm.at[3 * HD * h + HD : 3 * HD * (h + 1)],
                weight.at[PAIR * h : PAIR * (h + 1)],
            )
            for h in range(heads)
        ]
        + [(gain_hbm, gain.at[0]), (cache_hbm.at[: cache.shape[0]], cache)],
        sems,
    )
    for copy in copies[:5]:
        copy.wait()
    row = iota(owners.shape, 0)
    holders = jnp.full(owners.shape, requests, jnp.int32)
    left = jnp.zeros(owners.shape, jnp.int32)
    for b in range(blocks):
        holder = owner[0, b]
        most = jnp.where(holder < requests, length[jnp.minimum(holder, requests - 1)], 0)
        holders = jnp.where(row == b, holder, holders)
        left = jnp.where(row == b, most - index[0, b] * tokens, left)
    owners[...] = holders
    remains[...] = left
    start = place[1] * rows
    at_home = row_values(home, start, rows, 128)
    target = at_home ^ row_values(moving, start, rows, 128)
    homed[...] = jnp.where(at_home == place[0], 1.0, 0.0)
    serves = jnp.where(target == place[0], 1.0, 0.0)
    served[...] = serves
    for copy in copies[5:-1]:
        copy.wait()
    pairs = dot_transposed(normed[...], weight[...])
    entries[...] = jnp.where(widen(serves, pairs.shape[1]) > 0.0, pairs, 0.0)
    pair = pairs.astype(BF16).astype(F32)
    keys = jnp.concatenate([pair[:, PAIR * h : PAIR * h + HD] for h in range(heads)], axis=1)
    values[...] = jnp.concatenate(
        [pair[:, PAIR * h + HD : PAIR * (h + 1)] for h in range(heads)]
        + [jnp.zeros((rows, WIDE - heads * HD), F32)],
        axis=1,
    )
    product = query[...].astype(F32)[:, : heads * HD] * keys
    head_of = iota((rows, heads * HD), 1) // HD
    own_lane = iota((rows, 128), 1) - (STATS - 256)
    self_score = jnp.full((rows, 128), VERY_LOW, F32)
    for h in range(heads):
        score = jnp.sum(jnp.where(head_of == h, product, 0.0), axis=1, keepdims=True)
        self_score = jnp.where(own_lane == h, score, self_score)
    self_scores[...] = self_score
    copies[-1].wait()


def attend_kernel(
    owner_of, remains, queries, early, cache_hbm, out, late, parts, sums, sems
):
    blocks, tokens, width = cache_hbm.shape
    ready = early.shape[0]
    copies = fetch(
        [(cache_hbm.at[b], late.at[b - ready]) for b in range(ready, blocks)], sems
    )

    def cache(b):
        return early[b] if b < ready else late[b - ready]

    heads = width // PAIR
    requests = queries.shape[0]
    rows = sums.shape[0]
    onehot = (iota((rows, requests), 1) == widen(owner_of[...], requests)).astype(BF16)
    picked = jnp.dot(onehot, queries[...], preferred_element_type=F32)
    picked = jnp.concatenate([picked, jnp.zeros((rows, width - WIDE), F32)], axis=1)
    lane = iota((rows, width), 1)
    spread = jnp.zeros((rows, width), F32)
    for h in range(heads):
        moved = picked if h == 0 else pltpu.roll(picked, HD * h, 1)
        spread = jnp.where((lane >= PAIR * h) & (lane < PAIR * h + HD), moved, spread)
    head_lane = iota((8, width), 1) - PAIR * iota((8, width), 0)
    key_lanes = (head_lane >= 0) & (head_lane < HD)
    value_lanes = (head_lane >= HD) & (head_lane < PAIR)
    block_lane = iota((8, 128), 1)
    token_lane = iota((8, tokens), 1)
    every_peak = jnp.full((8, 128), VERY_LOW, F32)
    holders = jnp.full((8, 128), requests, jnp.int32)
    scores = [None] * blocks
    uses = [None] * blocks
    peaks = [None] * blocks
    totals = [None] * blocks

    def weigh(group):
        for b in group:
            peaks[b] = jnp.max(scores[b], axis=1, keepdims=True)
        for b in group:
            weights = jnp.where(uses[b], jnp.exp(scores[b] - peaks[b]), 0.0)
            totals[b] = jnp.sum(weights, axis=1, keepdims=True)
            acc = jnp.dot(weights.astype(BF16), cache(b), preferred_element_type=F32)
            parts[b] = jnp.where(value_lanes, acc, 0.0)

    before = ()
    starts = [0] + list(range(ready, blocks, LATE_GROUP)) + [blocks]
    for g in range(len(starts) - 1):
        group = range(starts[g], starts[g + 1])
        for b in group:
            if b >= ready:
                copies[b - ready].wait()
        for b in group:
            ask = jnp.where(key_lanes, jnp.broadcast_to(spread[b : b + 1], (8, width)), 0.0)
            score = dot_transposed(ask.astype(BF16), cache(b))
            left = widen(jnp.broadcast_to(remains[b : b + 1, :], (8, 128)), tokens)
            uses[b] = token_lane < left
            scores[b] = jnp.where(uses[b], score, VERY_LOW)
        weigh(before)
        before = group
    weigh(before)
    for b in range(blocks):
        every_peak = jnp.where(block_lane == b, peaks[b], every_peak)
        holders = jnp.where(block_lane == b, owner_of[b : b + 1, :], holders)
    stat_lane = iota((8, 128), 1) - (STATS - 256)
    stat_row = iota((8, 128), 0)
    stats = []
    for b in range(blocks):
        peers = jnp.where(holders == owner_of[b : b + 1, :], every_peak, VERY_LOW)
        joint = jnp.max(peers, axis=1, keepdims=True)
        factor = jnp.exp(peaks[b] - joint)
        sums[b : b + 1, :] = jnp.sum(parts[b] * factor, axis=0, keepdims=True)
        stat = jnp.where(stat_lane == stat_row, joint, 0.0)
        stat = stat + jnp.where(stat_lane == stat_row + 8, totals[b] * factor, 0.0)
        stats.append(jnp.sum(jnp.where(stat_row < heads, stat, 0.0), axis=0, keepdims=True))
    stats += [jnp.zeros((1, 128), F32)] * (rows - blocks)
    stats = jnp.concatenate(stats, axis=0)
    sums[blocks:rows, :] = jnp.zeros((rows - blocks, width), F32)
    packed = jnp.zeros((rows, width), F32)
    every = sums[...]
    for h in range(heads):
        moved = pltpu.roll(every, width - HD * (h + 1), 1)
        packed = jnp.where((lane >= HD * h) & (lane < HD * (h + 1)), moved, packed)
    packed = packed[:, :WIDE]
    added = jnp.zeros((rows, WIDE), F32)
    added_totals = jnp.zeros((rows, 128), F32)
    first = iota((rows, 128), 0) < blocks
    for b in range(blocks):
        same = owner_of[...] == owner_of[b : b + 1, :]
        added = added + jnp.where(widen(same, WIDE), packed[b : b + 1], 0.0)
        added_totals = added_totals + jnp.where(same, stats[b : b + 1], 0.0)
        first = first & ((iota((rows, 128), 0) <= b) | ~same)
    tail = iota((rows, 128), 1) - (STATS - 256)
    peak_part = jnp.where((tail >= 0) & (tail < 8), stats, 0.0)
    total_part = jnp.where((tail >= 8) & (tail < 16), added_totals, 0.0)
    terms = jnp.zeros((rows, 128), F32)
    for k, term in enumerate(split3(peak_part + total_part)):
        terms = terms + (term if k == 0 else pltpu.roll(term, 16 * k, 1))
    last = jnp.where(tail >= 0, terms, added[:, 256:])
    full = jnp.concatenate([added[:, :256], last], axis=1)
    keep = jnp.where(first, 1.0, 0.0)
    full = jnp.where(widen(keep, WIDE) > 0.0, full, 0.0).astype(BF16)
    out[...] = lax.dot_general(
        onehot,
        full,
        (((0,), (0,)), ((), ())),
        preferred_element_type=F32,
    ).astype(BF16)


def merge_kernel(shares, self_scores, values, attended):
    rows = values.shape[0]
    count = shares.shape[0] // rows
    heads = STATS // HD
    sums = shares[...].astype(F32)
    tail = sums[:, 256:]
    joined = tail + pltpu.roll(tail, 128 - 16, 1) + pltpu.roll(tail, 128 - 32, 1)
    totals = pltpu.roll(joined, 128 - 8, 1)
    lane = iota(joined.shape, 1) - (STATS - 256)
    peaks = jnp.where((lane >= 0) & (lane < heads) & (totals > 0.0), joined, VERY_LOW)
    self_score = self_scores[...]
    top = self_score
    for s in range(count):
        top = jnp.maximum(top, peaks[s * rows : (s + 1) * rows])
    denominator = jnp.exp(self_score - top)
    self_weight = denominator.astype(BF16).astype(F32)
    wide_of = iota((rows, WIDE), 1) // HD

    def per_head(value):
        out = jnp.zeros((rows, WIDE), F32)
        for h in range(heads):
            at = STATS - 256 + h
            out = jnp.where(wide_of == h, value[:, at : at + 1], out)
        return out

    numerator = per_head(self_weight) * values[...]
    for s in range(count):
        at = slice(s * rows, (s + 1) * rows)
        factor = jnp.exp(peaks[at] - top)
        denominator = denominator + factor * totals[at]
        numerator = numerator + per_head(factor) * sums[at]
    result = numerator / jnp.where(wide_of < heads, per_head(denominator), 1.0)
    attended[...] = result.astype(BF16)


def out_kernel(homed, here, there, weight, partial):
    stay = widen(homed[...], WIDE) > 0.0
    attended = jnp.where(stay, here[...].astype(F32), there[...].astype(F32)).astype(BF16)
    partial[...] = jnp.dot(
        attended[:, : weight.shape[0]], weight[...], preferred_element_type=F32
    ).astype(BF16)


def joined(own, near, across, far):
    own, near, across, far = (v[...].astype(F32) for v in (own, near, across, far))
    return (own + near) + (across + far)


def hidden_kernel(token, own, near, across, far, gain, up, down, residual, partial):
    total = token[...].astype(F32) + joined(own, near, across, far)
    residual[...] = total
    normed = root_norm(total, gain[...]).astype(BF16)
    hidden = dot_transposed(normed, up[...])
    active = jax.nn.gelu(hidden, approximate=True).astype(BF16)
    partial[...] = jnp.dot(active, down[...], preferred_element_type=F32).astype(BF16)


def finish_kernel(served, residual, own, near, across, far, out):
    result = residual[...] + joined(own, near, across, far)
    out[...] = jnp.where(widen(served[...], result.shape[1]) > 0.0, result, 0.0)


def shape(dims, dtype):
    return jax.ShapeDtypeStruct(dims, dtype)


def from_others(value):
    count = lax.axis_size("tp")
    return [
        lax.ppermute(value, "tp", [(i, i ^ bits) for i in range(count)])
        for bits in range(1, count)
    ]


def body(
    token_state,
    attn_gain,
    qkv_weight,
    out_weight,
    mlp_gain,
    up_weight,
    down_weight,
    kv_cache,
    home_replica,
    moving,
    cache_length,
    block_owner,
    block_index,
):
    rows, features = token_state.shape
    requests = home_replica.shape[0]
    _, blocks, tokens, width = kv_cache.shape
    heads = width // PAIR
    place = jnp.stack([lax.axis_index("rep"), lax.axis_index("kv")]).astype(jnp.int32)

    weight = qkv_weight.T
    spread, query, normed = pl.pallas_call(
        query_kernel,
        out_shape=(
            shape((requests, WIDE), BF16),
            shape((rows, WIDE), BF16),
            shape((rows, features), BF16),
        ),
        in_specs=[HBM] * 3,
        out_specs=(VMEM,) * 3,
        scratch_shapes=[
            pltpu.VMEM((rows, features), BF16),
            pltpu.VMEM((1, features), F32),
            pltpu.VMEM((WIDE, features), BF16),
            pltpu.SemaphoreType.DMA((2 + heads,)),
        ],
        compiler_params=PARAMS,
        name="query",
    )(*in_hbm(token_state, attn_gain, weight))
    queries = lax.all_to_all(spread, "kv", 0, 0, tiled=True)

    padded = -(-blocks // 16) * 16
    early, owners, remains, entries, homed, served, self_scores, values, gain = pl.pallas_call(
        side_kernel,
        out_shape=(
            pltpu.VMEM((EARLY, tokens, width), BF16),
            shape((padded, 128), jnp.int32),
            shape((padded, 128), jnp.int32),
            shape((rows, width), F32),
            shape((rows, 128), F32),
            shape((rows, 128), F32),
            shape((rows, 128), F32),
            shape((rows, WIDE), F32),
            shape((1, features), F32),
        ),
        in_specs=[SMEM] + [HBM] * 8 + [VMEM] * 2,
        out_specs=(VMEM,) * 9,
        scratch_shapes=[pltpu.SMEM((1, blocks), jnp.int32)] * 2
        + [pltpu.SMEM((requests,), jnp.int32)] * 3
        + [pltpu.VMEM((width, features), BF16), pltpu.SemaphoreType.DMA((7 + heads,))],
        compiler_params=PARAMS,
        cost_estimate=pl.CostEstimate(
            flops=0, bytes_accessed=2 * EARLY * tokens * width * 2, transcendentals=0
        ),
        name="side",
    )(
        place,
        *in_hbm(
            block_owner,
            block_index,
            cache_length,
            home_replica,
            moving,
            kv_cache[0],
            weight,
            mlp_gain,
        ),
        normed,
        query,
    )

    shares = pl.pallas_call(
        attend_kernel,
        out_shape=shape((requests, WIDE), BF16),
        in_specs=[VMEM] * 4 + [HBM],
        out_specs=VMEM,
        scratch_shapes=[
            pltpu.VMEM((blocks - EARLY, tokens, width), BF16),
            pltpu.VMEM((blocks, 8, width), F32),
            pltpu.VMEM((padded, width), F32),
            pltpu.SemaphoreType.DMA((blocks - EARLY,)),
        ],
        compiler_params=PARAMS,
        name="attend",
    )(
        owners,
        remains,
        queries,
        pltpu.with_memory_space_constraint(early, pltpu.VMEM),
        *in_hbm(kv_cache[0]),
    )
    shares = lax.all_to_all(shares, "kv", 0, 0, tiled=True)

    attended = pl.pallas_call(
        merge_kernel,
        out_shape=shape((rows, WIDE), BF16),
        in_specs=[VMEM] * 3,
        out_specs=VMEM,
        compiler_params=PARAMS,
        name="merge",
    )(shares, self_scores, values)
    other = lax.ppermute(attended, "rep", [(0, 1), (1, 0)])

    partial = pl.pallas_call(
        out_kernel,
        out_shape=shape((rows, features), BF16),
        in_specs=[VMEM] * 4,
        out_specs=VMEM,
        compiler_params=PARAMS,
        name="out_projection",
    )(homed, attended, other, out_weight)

    residual, partial = pl.pallas_call(
        hidden_kernel,
        out_shape=(shape((rows, features), F32), shape((rows, features), BF16)),
        in_specs=[VMEM] * 8,
        out_specs=(VMEM,) * 2,
        compiler_params=PARAMS,
        name="hidden",
    )(token_state, partial, *from_others(partial), gain, up_weight.T, down_weight)
    result = pl.pallas_call(
        finish_kernel,
        out_shape=shape((rows, features), F32),
        in_specs=[VMEM] * 6,
        out_specs=VMEM,
        compiler_params=PARAMS,
        name="finish",
    )(served, residual, partial, *from_others(partial))
    return (result[None], entries[None])


def solution(mesh):
    return jax.shard_map(
        body,
        mesh=mesh,
        in_specs=(
            P("kv", None),
            P(),
            P(None, "tp"),
            P("tp", None),
            P(),
            P(None, "tp"),
            P("tp", None),
            P("rep", "kv", None, "tp"),
            P(),
            P(),
            P(),
            P("rep", "kv"),
            P("rep", "kv"),
        ),
        out_specs=(P("rep", "kv", None), P("rep", "kv", "tp")),
        check_vma=False,
    )
```

```python
import functools

import jax
import jax.numpy as jnp
from jax import lax
from jax.experimental import pallas as pl
from jax.experimental.pallas import tpu as pltpu
from jax.sharding import PartitionSpec as P

HD = 80
PAIR = 2 * HD
VERY_LOW = -1e30
NORM_EPS = 1e-06
EARLY = 5
LATE_GROUP = 2
STATS = 320
WIDE = 384
F32 = jnp.float32
BF16 = jnp.bfloat16

VMEM = pl.BlockSpec(memory_space=pltpu.VMEM)
HBM = pl.BlockSpec(memory_space=pltpu.HBM)
PARAMS = pltpu.CompilerParams(vmem_limit_bytes=16 * 1024 * 1024)


def in_hbm(*arrays):
    return [pltpu.with_memory_space_constraint(a, pltpu.HBM) for a in arrays]


def iota(shape, axis):
    return lax.broadcasted_iota(jnp.int32, shape, axis)


def root_norm(values, gain):
    mean = jnp.mean(values * values, axis=-1, keepdims=True)
    return values * lax.rsqrt(mean + NORM_EPS) * gain


def row_values(ref, start, rows, lanes):
    row = iota((rows, lanes), 0)
    out = jnp.zeros((rows, lanes), jnp.int32)
    for r in range(rows):
        out = jnp.where(row == r, ref[start + r], out)
    return out


def widen(value, lanes):
    return jnp.concatenate([value] * (lanes // value.shape[1]), axis=1)


def split3(value):
    high = value.astype(BF16).astype(F32)
    rest = value - high
    middle = rest.astype(BF16).astype(F32)
    return high, middle, (rest - middle).astype(BF16).astype(F32)


def dot_transposed(left, right):
    return lax.dot_general(left, right, (((1,), (1,)), ((), ())), preferred_element_type=F32)


def fetch(pairs, sems):
    copies = [pltpu.make_async_copy(a, b, sems.at[i]) for i, (a, b) in enumerate(pairs)]
    for copy in copies:
        copy.start()
    return copies


def query_kernel(
    token_hbm, gain_hbm, weight_hbm, spread, query, normed, token, gain, weight, sems
):
    rows = token.shape[0]
    heads = weight_hbm.shape[0] // (3 * HD)
    copies = fetch(
        [
            (weight_hbm.at[3 * HD * h : 3 * HD * h + HD], weight.at[HD * h : HD * (h + 1)])
            for h in range(heads)
        ]
        + [(token_hbm, token), (gain_hbm, gain.at[0])],
        sems,
    )
    weight[heads * HD :, :] = jnp.zeros((WIDE - heads * HD, weight.shape[1]), BF16)
    copies[heads].wait()
    copies[heads + 1].wait()
    norm = root_norm(token[...].astype(F32), gain[...]).astype(BF16)
    normed[...] = norm
    for copy in copies[:heads]:
        copy.wait()
    own = (dot_transposed(norm, weight[...]) * HD ** (-0.5)).astype(BF16)
    query[...] = own
    for copy in range(spread.shape[0] // rows):
        spread[copy * rows : (copy + 1) * rows, :] = own


def side_kernel(
    owner_hbm,
    index_hbm,
    length_hbm,
    home_hbm,
    moving_hbm,
    cache_hbm,
    weight_hbm,
    gain_hbm,
    normed,
    query,
    cache,
    owners,
    remains,
    entries,
    homed,
    served,
    self_scores,
    values,
    gain,
    owner,
    index,
    length,
    home,
    moving,
    weight,
    sems,
):
    rows = normed.shape[0]
    blocks, tokens, _ = cache_hbm.shape
    heads = weight_hbm.shape[0] // (3 * HD)
    requests = length.shape[0]
    copies = fetch(
        [
            (owner_hbm, owner),
            (index_hbm, index),
            (length_hbm, length),
            (home_hbm, home),
            (moving_hbm, moving),
        ]
        + [
            (
                weight_hbm.at[3 * HD * h + HD : 3 * HD * (h + 1)],
                weight.at[PAIR * h : PAIR * (h + 1)],
            )
            for h in range(heads)
        ]
        + [(gain_hbm, gain.at[0]), (cache_hbm.at[: cache.shape[0]], cache)],
        sems,
    )
    for copy in copies[:5]:
        copy.wait()
    row = iota(owners.shape, 0)
    holders = jnp.full(owners.shape, requests, jnp.int32)
    left = jnp.zeros(owners.shape, jnp.int32)
    for b in range(blocks):
        holder = owner[0, b]
        most = jnp.where(holder < requests, length[jnp.minimum(holder, requests - 1)], 0)
        holders = jnp.where(row == b, holder, holders)
        left = jnp.where(row == b, most - index[0, b] * tokens, left)
    owners[...] = holders
    remains[...] = left
    start = lax.axis_index("kv") * rows
    replica = lax.axis_index("rep")
    at_home = row_values(home, start, rows, 128)
    target = at_home ^ row_values(moving, start, rows, 128)
    homed[...] = jnp.where(at_home == replica, 1.0, 0.0)
    serves = jnp.where(target == replica, 1.0, 0.0)
    served[...] = serves
    for copy in copies[5:-1]:
        copy.wait()
    pairs = dot_transposed(normed[...], weight[...])
    entries[...] = jnp.where(widen(serves, pairs.shape[1]) > 0.0, pairs, 0.0)
    pair = pairs.astype(BF16).astype(F32)
    keys = jnp.concatenate([pair[:, PAIR * h : PAIR * h + HD] for h in range(heads)], axis=1)
    values[...] = jnp.concatenate(
        [pair[:, PAIR * h + HD : PAIR * (h + 1)] for h in range(heads)]
        + [jnp.zeros((rows, WIDE - heads * HD), F32)],
        axis=1,
    )
    product = query[...].astype(F32)[:, : heads * HD] * keys
    head_of = iota((rows, heads * HD), 1) // HD
    own_lane = iota((rows, 128), 1) - (STATS - 256)
    self_score = jnp.full((rows, 128), VERY_LOW, F32)
    for h in range(heads):
        score = jnp.sum(jnp.where(head_of == h, product, 0.0), axis=1, keepdims=True)
        self_score = jnp.where(own_lane == h, score, self_score)
    self_scores[...] = self_score
    copies[-1].wait()


def attend_kernel(
    owner_of, remains, queries, early, cache_hbm, out, late, parts, sums, sems
):
    blocks, tokens, width = cache_hbm.shape
    ready = early.shape[0]
    copies = fetch(
        [(cache_hbm.at[b], late.at[b - ready]) for b in range(ready, blocks)], sems
    )

    def cache(b):
        return early[b] if b < ready else late[b - ready]

    heads = width // PAIR
    requests = queries.shape[0]
    rows = sums.shape[0]
    onehot = (iota((rows, requests), 1) == widen(owner_of[...], requests)).astype(BF16)
    picked = jnp.dot(onehot, queries[...], preferred_element_type=F32)
    picked = jnp.concatenate([picked, jnp.zeros((rows, width - WIDE), F32)], axis=1)
    lane = iota((rows, width), 1)
    spread = jnp.zeros((rows, width), F32)
    for h in range(heads):
        moved = picked if h == 0 else pltpu.roll(picked, HD * h, 1)
        spread = jnp.where((lane >= PAIR * h) & (lane < PAIR * h + HD), moved, spread)
    head_lane = iota((8, width), 1) - PAIR * iota((8, width), 0)
    key_lanes = (head_lane >= 0) & (head_lane < HD)
    value_lanes = (head_lane >= HD) & (head_lane < PAIR)
    block_lane = iota((8, 128), 1)
    token_lane = iota((8, tokens), 1)
    every_peak = jnp.full((8, 128), VERY_LOW, F32)
    holders = jnp.full((8, 128), requests, jnp.int32)
    scores = [None] * blocks
    uses = [None] * blocks
    peaks = [None] * blocks
    totals = [None] * blocks

    def weigh(group):
        for b in group:
            peaks[b] = jnp.max(scores[b], axis=1, keepdims=True)
        for b in group:
            weights = jnp.where(uses[b], jnp.exp(scores[b] - peaks[b]), 0.0)
            totals[b] = jnp.sum(weights, axis=1, keepdims=True)
            acc = jnp.dot(weights.astype(BF16), cache(b), preferred_element_type=F32)
            parts[b] = jnp.where(value_lanes, acc, 0.0)

    before = ()
    starts = [0] + list(range(ready, blocks, LATE_GROUP)) + [blocks]
    for g in range(len(starts) - 1):
        group = range(starts[g], starts[g + 1])
        for b in group:
            if b >= ready:
                copies[b - ready].wait()
        for b in group:
            ask = jnp.where(key_lanes, jnp.broadcast_to(spread[b : b + 1], (8, width)), 0.0)
            score = dot_transposed(ask.astype(BF16), cache(b))
            left = widen(jnp.broadcast_to(remains[b : b + 1, :], (8, 128)), tokens)
            uses[b] = token_lane < left
            scores[b] = jnp.where(uses[b], score, VERY_LOW)
        weigh(before)
        before = group
    weigh(before)
    for b in range(blocks):
        every_peak = jnp.where(block_lane == b, peaks[b], every_peak)
        holders = jnp.where(block_lane == b, owner_of[b : b + 1, :], holders)
    stat_lane = iota((8, 128), 1) - (STATS - 256)
    stat_row = iota((8, 128), 0)
    stats = []
    for b in range(blocks):
        peers = jnp.where(holders == owner_of[b : b + 1, :], every_peak, VERY_LOW)
        joint = jnp.max(peers, axis=1, keepdims=True)
        factor = jnp.exp(peaks[b] - joint)
        sums[b : b + 1, :] = jnp.sum(parts[b] * factor, axis=0, keepdims=True)
        stat = jnp.where(stat_lane == stat_row, joint, 0.0)
        stat = stat + jnp.where(stat_lane == stat_row + 8, totals[b] * factor, 0.0)
        stats.append(jnp.sum(jnp.where(stat_row < heads, stat, 0.0), axis=0, keepdims=True))
    stats += [jnp.zeros((1, 128), F32)] * (rows - blocks)
    stats = jnp.concatenate(stats, axis=0)
    sums[blocks:rows, :] = jnp.zeros((rows - blocks, width), F32)
    packed = jnp.zeros((rows, width), F32)
    every = sums[...]
    for h in range(heads):
        moved = pltpu.roll(every, width - HD * (h + 1), 1)
        packed = jnp.where((lane >= HD * h) & (lane < HD * (h + 1)), moved, packed)
    packed = packed[:, :WIDE]
    added = jnp.zeros((rows, WIDE), F32)
    added_totals = jnp.zeros((rows, 128), F32)
    first = iota((rows, 128), 0) < blocks
    for b in range(blocks):
        same = owner_of[...] == owner_of[b : b + 1, :]
        added = added + jnp.where(widen(same, WIDE), packed[b : b + 1], 0.0)
        added_totals = added_totals + jnp.where(same, stats[b : b + 1], 0.0)
        first = first & ((iota((rows, 128), 0) <= b) | ~same)
    tail = iota((rows, 128), 1) - (STATS - 256)
    peak_part = jnp.where((tail >= 0) & (tail < 8), stats, 0.0)
    total_part = jnp.where((tail >= 8) & (tail < 16), added_totals, 0.0)
    terms = jnp.zeros((rows, 128), F32)
    for k, term in enumerate(split3(peak_part + total_part)):
        terms = terms + (term if k == 0 else pltpu.roll(term, 16 * k, 1))
    last = jnp.where(tail >= 0, terms, added[:, 256:])
    full = jnp.concatenate([added[:, :256], last], axis=1)
    keep = jnp.where(first, 1.0, 0.0)
    full = jnp.where(widen(keep, WIDE) > 0.0, full, 0.0).astype(BF16)
    out[...] = lax.dot_general(
        onehot,
        full,
        (((0,), (0,)), ((), ())),
        preferred_element_type=F32,
    ).astype(BF16)


def merge_kernel(shares, self_scores, values, attended):
    rows = values.shape[0]
    count = shares.shape[0] // rows
    heads = STATS // HD
    sums = shares[...].astype(F32)
    tail = sums[:, 256:]
    joined = tail + pltpu.roll(tail, 128 - 16, 1) + pltpu.roll(tail, 128 - 32, 1)
    totals = pltpu.roll(joined, 128 - 8, 1)
    lane = iota(joined.shape, 1) - (STATS - 256)
    peaks = jnp.where((lane >= 0) & (lane < heads) & (totals > 0.0), joined, VERY_LOW)
    self_score = self_scores[...]
    top = self_score
    for s in range(count):
        top = jnp.maximum(top, peaks[s * rows : (s + 1) * rows])
    denominator = jnp.exp(self_score - top)
    self_weight = denominator.astype(BF16).astype(F32)
    wide_of = iota((rows, WIDE), 1) // HD

    def per_head(value):
        out = jnp.zeros((rows, WIDE), F32)
        for h in range(heads):
            at = STATS - 256 + h
            out = jnp.where(wide_of == h, value[:, at : at + 1], out)
        return out

    numerator = per_head(self_weight) * values[...]
    for s in range(count):
        at = slice(s * rows, (s + 1) * rows)
        factor = jnp.exp(peaks[at] - top)
        denominator = denominator + factor * totals[at]
        numerator = numerator + per_head(factor) * sums[at]
    result = numerator / jnp.where(wide_of < heads, per_head(denominator), 1.0)
    attended[...] = result.astype(BF16)


def out_kernel(homed, here, there, weight, partial):
    stay = widen(homed[...], WIDE) > 0.0
    attended = jnp.where(stay, here[...].astype(F32), there[...].astype(F32)).astype(BF16)
    partial[...] = jnp.dot(
        attended[:, : weight.shape[0]], weight[...], preferred_element_type=F32
    ).astype(BF16)


def joined(own, near, across, far):
    own, near, across, far = (v[...].astype(F32) for v in (own, near, across, far))
    return (own + near) + (across + far)


def hidden_kernel(token, own, near, far, across, gain, up, down, residual, partial):
    total = token[...].astype(F32) + joined(own, near, across, far)
    residual[...] = total
    normed = root_norm(total, gain[...]).astype(BF16)
    hidden = dot_transposed(normed, up[...])
    active = jax.nn.gelu(hidden, approximate=True).astype(BF16)
    partial[...] = jnp.dot(active, down[...], preferred_element_type=F32).astype(BF16)


def finish_kernel(served, residual, own, near, far, across, out):
    result = residual[...] + joined(own, near, across, far)
    out[...] = jnp.where(widen(served[...], result.shape[1]) > 0.0, result, 0.0)


def shape(dims, dtype):
    return jax.ShapeDtypeStruct(dims, dtype)


def from_others(value):
    count = lax.axis_size("tp")
    return [
        lax.ppermute(value, "tp", [(i, i ^ bits) for i in range(count)])
        for bits in (1, 3, 2)
    ]


def body(
    token_state,
    attn_gain,
    qkv_weight,
    out_weight,
    mlp_gain,
    up_weight,
    down_weight,
    kv_cache,
    home_replica,
    moving,
    cache_length,
    block_owner,
    block_index,
):
    rows, features = token_state.shape
    requests = home_replica.shape[0]
    _, blocks, tokens, width = kv_cache.shape
    heads = width // PAIR

    weight = qkv_weight.T
    spread, query, normed = pl.pallas_call(
        query_kernel,
        out_shape=(
            shape((requests, WIDE), BF16),
            shape((rows, WIDE), BF16),
            shape((rows, features), BF16),
        ),
        in_specs=[HBM] * 3,
        out_specs=(VMEM,) * 3,
        scratch_shapes=[
            pltpu.VMEM((rows, features), BF16),
            pltpu.VMEM((1, features), F32),
            pltpu.VMEM((WIDE, features), BF16),
            pltpu.SemaphoreType.DMA((2 + heads,)),
        ],
        compiler_params=PARAMS,
        name="query",
    )(*in_hbm(token_state, attn_gain, weight))
    queries = lax.all_to_all(spread, "kv", 0, 0, tiled=True)

    padded = -(-blocks // 16) * 16
    early, owners, remains, entries, homed, served, self_scores, values, gain = pl.pallas_call(
        side_kernel,
        out_shape=(
            pltpu.VMEM((EARLY, tokens, width), BF16),
            shape((padded, 128), jnp.int32),
            shape((padded, 128), jnp.int32),
            shape((rows, width), F32),
            shape((rows, 128), F32),
            shape((rows, 128), F32),
            shape((rows, 128), F32),
            shape((rows, WIDE), F32),
            shape((1, features), F32),
        ),
        in_specs=[HBM] * 8 + [VMEM] * 2,
        out_specs=(VMEM,) * 9,
        scratch_shapes=[pltpu.SMEM((1, blocks), jnp.int32)] * 2
        + [pltpu.SMEM((requests,), jnp.int32)] * 3
        + [pltpu.VMEM((width, features), BF16), pltpu.SemaphoreType.DMA((7 + heads,))],
        compiler_params=PARAMS,
        cost_estimate=pl.CostEstimate(
            flops=0, bytes_accessed=2 * EARLY * tokens * width * 2, transcendentals=0
        ),
        name="side",
    )(
        *in_hbm(
            block_owner,
            block_index,
            cache_length,
            home_replica,
            moving,
            kv_cache[0],
            weight,
            mlp_gain,
        ),
        normed,
        query,
    )

    shares = pl.pallas_call(
        attend_kernel,
        out_shape=shape((requests, WIDE), BF16),
        in_specs=[VMEM] * 4 + [HBM],
        out_specs=VMEM,
        scratch_shapes=[
            pltpu.VMEM((blocks - EARLY, tokens, width), BF16),
            pltpu.VMEM((blocks, 8, width), F32),
            pltpu.VMEM((padded, width), F32),
            pltpu.SemaphoreType.DMA((blocks - EARLY,)),
        ],
        compiler_params=PARAMS,
        name="attend",
    )(
        owners,
        remains,
        queries,
        pltpu.with_memory_space_constraint(early, pltpu.VMEM),
        *in_hbm(kv_cache[0]),
    )
    shares = lax.all_to_all(shares, "kv", 0, 0, tiled=True)

    attended = pl.pallas_call(
        merge_kernel,
        out_shape=shape((rows, WIDE), BF16),
        in_specs=[VMEM] * 3,
        out_specs=VMEM,
        compiler_params=PARAMS,
        name="merge",
    )(shares, self_scores, values)
    other = lax.ppermute(attended, "rep", [(0, 1), (1, 0)])

    partial = pl.pallas_call(
        out_kernel,
        out_shape=shape((rows, features), BF16),
        in_specs=[VMEM] * 4,
        out_specs=VMEM,
        compiler_params=PARAMS,
        name="out_projection",
    )(homed, attended, other, out_weight)

    residual, partial = pl.pallas_call(
        hidden_kernel,
        out_shape=(shape((rows, features), F32), shape((rows, features), BF16)),
        in_specs=[VMEM] * 8,
        out_specs=(VMEM,) * 2,
        compiler_params=PARAMS,
        name="hidden",
    )(token_state, partial, *from_others(partial), gain, up_weight.T, down_weight)
    result = pl.pallas_call(
        finish_kernel,
        out_shape=shape((rows, features), F32),
        in_specs=[VMEM] * 6,
        out_specs=VMEM,
        compiler_params=PARAMS,
        name="finish",
    )(served, residual, partial, *from_others(partial))
    return (result[None], entries[None])


def solution(mesh):
    return jax.shard_map(
        body,
        mesh=mesh,
        in_specs=(
            P("kv", None),
            P(),
            P(None, "tp"),
            P("tp", None),
            P(),
            P(None, "tp"),
            P("tp", None),
            P("rep", "kv", None, "tp"),
            P(),
            P(),
            P(),
            P("rep", "kv"),
            P("rep", "kv"),
        ),
        out_specs=(P("rep", "kv", None), P("rep", "kv", "tp")),
        check_vma=False,
    )
```

```python
import functools

import jax
import jax.numpy as jnp
from jax import lax
from jax.experimental import pallas as pl
from jax.experimental.pallas import tpu as pltpu
from jax.sharding import PartitionSpec as P

HD = 80
PAIR = 2 * HD
VERY_LOW = -1e30
NORM_EPS = 1e-06
EARLY = 5
LATE_GROUP = 2
STATS = 320
WIDE = 384
F32 = jnp.float32
BF16 = jnp.bfloat16

VMEM = pl.BlockSpec(memory_space=pltpu.VMEM)
HBM = pl.BlockSpec(memory_space=pltpu.HBM)
PARAMS = pltpu.CompilerParams(vmem_limit_bytes=16 * 1024 * 1024)


def in_hbm(*arrays):
    return [pltpu.with_memory_space_constraint(a, pltpu.HBM) for a in arrays]


def iota(shape, axis):
    return lax.broadcasted_iota(jnp.int32, shape, axis)


def root_norm(values, gain):
    mean = jnp.mean(values * values, axis=-1, keepdims=True)
    return values * lax.rsqrt(mean + NORM_EPS) * gain


def row_values(ref, start, rows, lanes):
    row = iota((rows, lanes), 0)
    out = jnp.zeros((rows, lanes), jnp.int32)
    for r in range(rows):
        out = jnp.where(row == r, ref[start + r], out)
    return out


def widen(value, lanes):
    return jnp.concatenate([value] * (lanes // value.shape[1]), axis=1)


def split3(value):
    high = value.astype(BF16).astype(F32)
    rest = value - high
    middle = rest.astype(BF16).astype(F32)
    return high, middle, (rest - middle).astype(BF16).astype(F32)


def dot_transposed(left, right):
    return lax.dot_general(left, right, (((1,), (1,)), ((), ())), preferred_element_type=F32)


def fetch(pairs, sems):
    copies = [pltpu.make_async_copy(a, b, sems.at[i]) for i, (a, b) in enumerate(pairs)]
    for copy in copies:
        copy.start()
    return copies


def query_kernel(
    token_hbm, gain_hbm, weight_hbm, spread, query, normed, token, gain, weight, sems
):
    rows = token.shape[0]
    heads = weight_hbm.shape[0] // (3 * HD)
    copies = fetch(
        [
            (weight_hbm.at[3 * HD * h : 3 * HD * h + HD], weight.at[HD * h : HD * (h + 1)])
            for h in range(heads)
        ]
        + [(token_hbm, token), (gain_hbm, gain.at[0])],
        sems,
    )
    weight[heads * HD :, :] = jnp.zeros((WIDE - heads * HD, weight.shape[1]), BF16)
    copies[heads].wait()
    copies[heads + 1].wait()
    norm = root_norm(token[...].astype(F32), gain[...]).astype(BF16)
    normed[...] = norm
    for copy in copies[:heads]:
        copy.wait()
    own = (dot_transposed(norm, weight[...]) * HD ** (-0.5)).astype(BF16)
    query[...] = own
    for copy in range(spread.shape[0] // rows):
        spread[copy * rows : (copy + 1) * rows, :] = own


def side_kernel(
    owner_hbm,
    index_hbm,
    length_hbm,
    home_hbm,
    moving_hbm,
    cache_hbm,
    weight_hbm,
    gain_hbm,
    normed,
    query,
    cache,
    owners,
    remains,
    entries,
    homed,
    served,
    self_scores,
    values,
    gain,
    owner,
    index,
    length,
    home,
    moving,
    weight,
    sems,
):
    rows = normed.shape[0]
    blocks, tokens, _ = cache_hbm.shape
    heads = weight_hbm.shape[0] // (3 * HD)
    requests = length.shape[0]
    copies = fetch(
        [
            (owner_hbm, owner),
            (index_hbm, index),
            (length_hbm, length),
            (home_hbm, home),
            (moving_hbm, moving),
        ]
        + [
            (
                weight_hbm.at[3 * HD * h + HD : 3 * HD * (h + 1)],
                weight.at[PAIR * h : PAIR * (h + 1)],
            )
            for h in range(heads)
        ]
        + [(gain_hbm, gain.at[0]), (cache_hbm.at[: cache.shape[0]], cache)],
        sems,
    )
    for copy in copies[:5]:
        copy.wait()
    row = iota(owners.shape, 0)
    holders = jnp.full(owners.shape, requests, jnp.int32)
    left = jnp.zeros(owners.shape, jnp.int32)
    for b in range(blocks):
        holder = owner[0, b]
        most = jnp.where(holder < requests, length[jnp.minimum(holder, requests - 1)], 0)
        holders = jnp.where(row == b, holder, holders)
        left = jnp.where(row == b, most - index[0, b] * tokens, left)
    owners[...] = holders
    remains[...] = left
    start = lax.axis_index("kv") * rows
    replica = lax.axis_index("rep")
    at_home = row_values(home, start, rows, 128)
    target = at_home ^ row_values(moving, start, rows, 128)
    homed[...] = jnp.where(at_home == replica, 1.0, 0.0)
    serves = jnp.where(target == replica, 1.0, 0.0)
    served[...] = serves
    for copy in copies[5:-1]:
        copy.wait()
    pairs = dot_transposed(normed[...], weight[...])
    entries[...] = jnp.where(widen(serves, pairs.shape[1]) > 0.0, pairs, 0.0)
    pair = pairs.astype(BF16).astype(F32)
    keys = jnp.concatenate([pair[:, PAIR * h : PAIR * h + HD] for h in range(heads)], axis=1)
    values[...] = jnp.concatenate(
        [pair[:, PAIR * h + HD : PAIR * (h + 1)] for h in range(heads)]
        + [jnp.zeros((rows, WIDE - heads * HD), F32)],
        axis=1,
    )
    product = query[...].astype(F32)[:, : heads * HD] * keys
    head_of = iota((rows, heads * HD), 1) // HD
    own_lane = iota((rows, 128), 1) - (STATS - 256)
    self_score = jnp.full((rows, 128), VERY_LOW, F32)
    for h in range(heads):
        score = jnp.sum(jnp.where(head_of == h, product, 0.0), axis=1, keepdims=True)
        self_score = jnp.where(own_lane == h, score, self_score)
    self_scores[...] = self_score
    copies[-1].wait()


def attend_kernel(
    owner_of, remains, queries, early, cache_hbm, out, late, parts, sums, sems
):
    blocks, tokens, width = cache_hbm.shape
    ready = early.shape[0]
    copies = fetch(
        [(cache_hbm.at[b], late.at[b - ready]) for b in range(ready, blocks)], sems
    )

    def cache(b):
        return early[b] if b < ready else late[b - ready]

    heads = width // PAIR
    requests = queries.shape[0]
    rows = sums.shape[0]
    onehot = (iota((rows, requests), 1) == widen(owner_of[...], requests)).astype(BF16)
    picked = jnp.dot(onehot, queries[...], preferred_element_type=F32)
    picked = jnp.concatenate([picked, jnp.zeros((rows, width - WIDE), F32)], axis=1)
    lane = iota((rows, width), 1)
    spread = jnp.zeros((rows, width), F32)
    for h in range(heads):
        moved = picked if h == 0 else pltpu.roll(picked, HD * h, 1)
        spread = jnp.where((lane >= PAIR * h) & (lane < PAIR * h + HD), moved, spread)
    head_lane = iota((8, width), 1) - PAIR * iota((8, width), 0)
    key_lanes = (head_lane >= 0) & (head_lane < HD)
    value_lanes = (head_lane >= HD) & (head_lane < PAIR)
    block_lane = iota((8, 128), 1)
    token_lane = iota((8, tokens), 1)
    every_peak = jnp.full((8, 128), VERY_LOW, F32)
    holders = jnp.full((8, 128), requests, jnp.int32)
    scores = [None] * blocks
    uses = [None] * blocks
    peaks = [None] * blocks
    totals = [None] * blocks

    def weigh(group):
        for b in group:
            peaks[b] = jnp.max(scores[b], axis=1, keepdims=True)
        for b in group:
            weights = jnp.where(uses[b], jnp.exp(scores[b] - peaks[b]), 0.0)
            totals[b] = jnp.sum(weights, axis=1, keepdims=True)
            acc = jnp.dot(weights.astype(BF16), cache(b), preferred_element_type=F32)
            parts[b] = jnp.where(value_lanes, acc, 0.0)

    before = ()
    starts = [0] + list(range(ready, blocks, LATE_GROUP)) + [blocks]
    for g in range(len(starts) - 1):
        group = range(starts[g], starts[g + 1])
        for b in group:
            if b >= ready:
                copies[b - ready].wait()
        for b in group:
            ask = jnp.where(key_lanes, jnp.broadcast_to(spread[b : b + 1], (8, width)), 0.0)
            score = dot_transposed(ask.astype(BF16), cache(b))
            left = widen(jnp.broadcast_to(remains[b : b + 1, :], (8, 128)), tokens)
            uses[b] = token_lane < left
            scores[b] = jnp.where(uses[b], score, VERY_LOW)
        weigh(before)
        before = group
    weigh(before)
    for b in range(blocks):
        every_peak = jnp.where(block_lane == b, peaks[b], every_peak)
        holders = jnp.where(block_lane == b, owner_of[b : b + 1, :], holders)
    every_joint = every_peak
    for b in range(blocks):
        peer = jnp.where(holders == owner_of[b : b + 1, :], peaks[b], VERY_LOW)
        every_joint = jnp.maximum(every_joint, peer)
    every_factor = jnp.exp(every_peak - every_joint)
    stat_lane = iota((8, 128), 1) - (STATS - 256)
    stat_row = iota((8, 128), 0)
    stats = []
    for b in range(blocks):
        joint = every_joint[:, b : b + 1]
        factor = every_factor[:, b : b + 1]
        sums[b : b + 1, :] = jnp.sum(parts[b] * factor, axis=0, keepdims=True)
        stat = jnp.where(stat_lane == stat_row, joint, 0.0)
        stat = stat + jnp.where(stat_lane == stat_row + 8, totals[b] * factor, 0.0)
        stats.append(jnp.sum(jnp.where(stat_row < heads, stat, 0.0), axis=0, keepdims=True))
    stats += [jnp.zeros((1, 128), F32)] * (rows - blocks)
    stats = jnp.concatenate(stats, axis=0)
    sums[blocks:rows, :] = jnp.zeros((rows - blocks, width), F32)
    packed = jnp.zeros((rows, width), F32)
    every = sums[...]
    for h in range(heads):
        moved = pltpu.roll(every, width - HD * (h + 1), 1)
        packed = jnp.where((lane >= HD * h) & (lane < HD * (h + 1)), moved, packed)
    packed = packed[:, :WIDE]
    added = jnp.zeros((rows, WIDE), F32)
    added_totals = jnp.zeros((rows, 128), F32)
    first = iota((rows, 128), 0) < blocks
    for b in range(blocks):
        same = owner_of[...] == owner_of[b : b + 1, :]
        added = added + jnp.where(widen(same, WIDE), packed[b : b + 1], 0.0)
        added_totals = added_totals + jnp.where(same, stats[b : b + 1], 0.0)
        first = first & ((iota((rows, 128), 0) <= b) | ~same)
    tail = iota((rows, 128), 1) - (STATS - 256)
    peak_part = jnp.where((tail >= 0) & (tail < 8), stats, 0.0)
    total_part = jnp.where((tail >= 8) & (tail < 16), added_totals, 0.0)
    terms = jnp.zeros((rows, 128), F32)
    for k, term in enumerate(split3(peak_part + total_part)):
        terms = terms + (term if k == 0 else pltpu.roll(term, 16 * k, 1))
    last = jnp.where(tail >= 0, terms, added[:, 256:])
    full = jnp.concatenate([added[:, :256], last], axis=1)
    keep = jnp.where(first, 1.0, 0.0)
    full = jnp.where(widen(keep, WIDE) > 0.0, full, 0.0).astype(BF16)
    out[...] = lax.dot_general(
        onehot,
        full,
        (((0,), (0,)), ((), ())),
        preferred_element_type=F32,
    ).astype(BF16)


def merge_kernel(shares, self_scores, values, attended):
    rows = values.shape[0]
    count = shares.shape[0] // rows
    heads = STATS // HD
    sums = shares[...].astype(F32)
    tail = sums[:, 256:]
    joined = tail + pltpu.roll(tail, 128 - 16, 1) + pltpu.roll(tail, 128 - 32, 1)
    totals = pltpu.roll(joined, 128 - 8, 1)
    lane = iota(joined.shape, 1) - (STATS - 256)
    peaks = jnp.where((lane >= 0) & (lane < heads) & (totals > 0.0), joined, VERY_LOW)
    self_score = self_scores[...]
    top = self_score
    for s in range(count):
        top = jnp.maximum(top, peaks[s * rows : (s + 1) * rows])
    denominator = jnp.exp(self_score - top)
    self_weight = denominator.astype(BF16).astype(F32)
    wide_of = iota((rows, WIDE), 1) // HD

    def per_head(value):
        out = jnp.zeros((rows, WIDE), F32)
        for h in range(heads):
            at = STATS - 256 + h
            out = jnp.where(wide_of == h, value[:, at : at + 1], out)
        return out

    numerator = per_head(self_weight) * values[...]
    for s in range(count):
        at = slice(s * rows, (s + 1) * rows)
        factor = jnp.exp(peaks[at] - top)
        denominator = denominator + factor * totals[at]
        numerator = numerator + per_head(factor) * sums[at]
    result = numerator / jnp.where(wide_of < heads, per_head(denominator), 1.0)
    attended[...] = result.astype(BF16)


def out_kernel(homed, here, there, weight, partial):
    stay = widen(homed[...], WIDE) > 0.0
    attended = jnp.where(stay, here[...].astype(F32), there[...].astype(F32)).astype(BF16)
    partial[...] = jnp.dot(
        attended[:, : weight.shape[0]], weight[...], preferred_element_type=F32
    ).astype(BF16)


def joined(own, near, across, far):
    own, near, across, far = (v[...].astype(F32) for v in (own, near, across, far))
    return (own + near) + (across + far)


def hidden_kernel(token, own, near, far, across, gain, up, down, residual, partial):
    total = token[...].astype(F32) + joined(own, near, across, far)
    residual[...] = total
    normed = root_norm(total, gain[...]).astype(BF16)
    hidden = dot_transposed(normed, up[...])
    active = jax.nn.gelu(hidden, approximate=True).astype(BF16)
    partial[...] = jnp.dot(active, down[...], preferred_element_type=F32).astype(BF16)


def finish_kernel(served, residual, own, near, far, across, out):
    result = residual[...] + joined(own, near, across, far)
    out[...] = jnp.where(widen(served[...], result.shape[1]) > 0.0, result, 0.0)


def shape(dims, dtype):
    return jax.ShapeDtypeStruct(dims, dtype)


def from_others(value):
    count = lax.axis_size("tp")
    return [
        lax.ppermute(value, "tp", [(i, i ^ bits) for i in range(count)])
        for bits in (1, 3, 2)
    ]


def body(
    token_state,
    attn_gain,
    qkv_weight,
    out_weight,
    mlp_gain,
    up_weight,
    down_weight,
    kv_cache,
    home_replica,
    moving,
    cache_length,
    block_owner,
    block_index,
):
    rows, features = token_state.shape
    requests = home_replica.shape[0]
    _, blocks, tokens, width = kv_cache.shape
    heads = width // PAIR

    weight = qkv_weight.T
    spread, query, normed = pl.pallas_call(
        query_kernel,
        out_shape=(
            shape((requests, WIDE), BF16),
            shape((rows, WIDE), BF16),
            shape((rows, features), BF16),
        ),
        in_specs=[HBM] * 3,
        out_specs=(VMEM,) * 3,
        scratch_shapes=[
            pltpu.VMEM((rows, features), BF16),
            pltpu.VMEM((1, features), F32),
            pltpu.VMEM((WIDE, features), BF16),
            pltpu.SemaphoreType.DMA((2 + heads,)),
        ],
        compiler_params=PARAMS,
        name="query",
    )(*in_hbm(token_state, attn_gain, weight))
    queries = lax.all_to_all(spread, "kv", 0, 0, tiled=True)

    padded = -(-blocks // 16) * 16
    early, owners, remains, entries, homed, served, self_scores, values, gain = pl.pallas_call(
        side_kernel,
        out_shape=(
            pltpu.VMEM((EARLY, tokens, width), BF16),
            shape((padded, 128), jnp.int32),
            shape((padded, 128), jnp.int32),
            shape((rows, width), F32),
            shape((rows, 128), F32),
            shape((rows, 128), F32),
            shape((rows, 128), F32),
            shape((rows, WIDE), F32),
            shape((1, features), F32),
        ),
        in_specs=[HBM] * 8 + [VMEM] * 2,
        out_specs=(VMEM,) * 9,
        scratch_shapes=[pltpu.SMEM((1, blocks), jnp.int32)] * 2
        + [pltpu.SMEM((requests,), jnp.int32)] * 3
        + [pltpu.VMEM((width, features), BF16), pltpu.SemaphoreType.DMA((7 + heads,))],
        compiler_params=PARAMS,
        cost_estimate=pl.CostEstimate(
            flops=0, bytes_accessed=2 * EARLY * tokens * width * 2, transcendentals=0
        ),
        name="side",
    )(
        *in_hbm(
            block_owner,
            block_index,
            cache_length,
            home_replica,
            moving,
            kv_cache[0],
            weight,
            mlp_gain,
        ),
        normed,
        query,
    )

    shares = pl.pallas_call(
        attend_kernel,
        out_shape=shape((requests, WIDE), BF16),
        in_specs=[VMEM] * 4 + [HBM],
        out_specs=VMEM,
        scratch_shapes=[
            pltpu.VMEM((blocks - EARLY, tokens, width), BF16),
            pltpu.VMEM((blocks, 8, width), F32),
            pltpu.VMEM((padded, width), F32),
            pltpu.SemaphoreType.DMA((blocks - EARLY,)),
        ],
        compiler_params=PARAMS,
        name="attend",
    )(
        owners,
        remains,
        queries,
        pltpu.with_memory_space_constraint(early, pltpu.VMEM),
        *in_hbm(kv_cache[0]),
    )
    shares = lax.all_to_all(shares, "kv", 0, 0, tiled=True)

    attended = pl.pallas_call(
        merge_kernel,
        out_shape=shape((rows, WIDE), BF16),
        in_specs=[VMEM] * 3,
        out_specs=VMEM,
        compiler_params=PARAMS,
        name="merge",
    )(shares, self_scores, values)
    other = lax.ppermute(attended, "rep", [(0, 1), (1, 0)])

    partial = pl.pallas_call(
        out_kernel,
        out_shape=shape((rows, features), BF16),
        in_specs=[VMEM] * 4,
        out_specs=VMEM,
        compiler_params=PARAMS,
        name="out_projection",
    )(homed, attended, other, out_weight)

    residual, partial = pl.pallas_call(
        hidden_kernel,
        out_shape=(shape((rows, features), F32), shape((rows, features), BF16)),
        in_specs=[VMEM] * 8,
        out_specs=(VMEM,) * 2,
        compiler_params=PARAMS,
        name="hidden",
    )(token_state, partial, *from_others(partial), gain, up_weight.T, down_weight)
    result = pl.pallas_call(
        finish_kernel,
        out_shape=shape((rows, features), F32),
        in_specs=[VMEM] * 6,
        out_specs=VMEM,
        compiler_params=PARAMS,
        name="finish",
    )(served, residual, partial, *from_others(partial))
    return (result[None], entries[None])


def solution(mesh):
    return jax.shard_map(
        body,
        mesh=mesh,
        in_specs=(
            P("kv", None),
            P(),
            P(None, "tp"),
            P("tp", None),
            P(),
            P(None, "tp"),
            P("tp", None),
            P("rep", "kv", None, "tp"),
            P(),
            P(),
            P(),
            P("rep", "kv"),
            P("rep", "kv"),
        ),
        out_specs=(P("rep", "kv", None), P("rep", "kv", "tp")),
        check_vma=False,
    )
```

```python
import functools

import jax
import jax.numpy as jnp
from jax import lax
from jax.experimental import pallas as pl
from jax.experimental.pallas import tpu as pltpu
from jax.sharding import PartitionSpec as P

HD = 80
PAIR = 2 * HD
VERY_LOW = -1e30
NORM_EPS = 1e-06
EARLY = 5
LATE_GROUP = 2
STATS = 320
WIDE = 384
F32 = jnp.float32
BF16 = jnp.bfloat16

VMEM = pl.BlockSpec(memory_space=pltpu.VMEM)
HBM = pl.BlockSpec(memory_space=pltpu.HBM)
PARAMS = pltpu.CompilerParams(vmem_limit_bytes=16 * 1024 * 1024)


def in_hbm(*arrays):
    return [pltpu.with_memory_space_constraint(a, pltpu.HBM) for a in arrays]


def iota(shape, axis):
    return lax.broadcasted_iota(jnp.int32, shape, axis)


def root_norm(values, gain):
    mean = jnp.mean(values * values, axis=-1, keepdims=True)
    return values * lax.rsqrt(mean + NORM_EPS) * gain


def row_values(ref, start, rows, lanes):
    row = iota((rows, lanes), 0)
    out = jnp.zeros((rows, lanes), jnp.int32)
    for r in range(rows):
        out = jnp.where(row == r, ref[start + r], out)
    return out


def widen(value, lanes):
    return jnp.concatenate([value] * (lanes // value.shape[1]), axis=1)


def split3(value):
    high = value.astype(BF16).astype(F32)
    rest = value - high
    middle = rest.astype(BF16).astype(F32)
    return high, middle, (rest - middle).astype(BF16).astype(F32)


def dot_transposed(left, right):
    return lax.dot_general(left, right, (((1,), (1,)), ((), ())), preferred_element_type=F32)


def fetch(pairs, sems):
    copies = [pltpu.make_async_copy(a, b, sems.at[i]) for i, (a, b) in enumerate(pairs)]
    for copy in copies:
        copy.start()
    return copies


def query_kernel(
    token_hbm, gain_hbm, weight_hbm, spread, query, normed, token, gain, weight, sems
):
    rows = token.shape[0]
    heads = weight_hbm.shape[0] // (3 * HD)
    copies = fetch(
        [
            (weight_hbm.at[3 * HD * h : 3 * HD * h + HD], weight.at[HD * h : HD * (h + 1)])
            for h in range(heads)
        ]
        + [(token_hbm, token), (gain_hbm, gain.at[0])],
        sems,
    )
    weight[heads * HD :, :] = jnp.zeros((WIDE - heads * HD, weight.shape[1]), BF16)
    copies[heads].wait()
    copies[heads + 1].wait()
    norm = root_norm(token[...].astype(F32), gain[...]).astype(BF16)
    normed[...] = norm
    for copy in copies[:heads]:
        copy.wait()
    own = (dot_transposed(norm, weight[...]) * HD ** (-0.5)).astype(BF16)
    query[...] = own
    for copy in range(spread.shape[0] // rows):
        spread[copy * rows : (copy + 1) * rows, :] = own


def side_kernel(
    owner_hbm,
    index_hbm,
    length_hbm,
    home_hbm,
    moving_hbm,
    cache_hbm,
    weight_hbm,
    gain_hbm,
    normed,
    query,
    cache,
    owners,
    remains,
    entries,
    homed,
    served,
    self_scores,
    values,
    gain,
    owner,
    index,
    length,
    home,
    moving,
    weight,
    sems,
):
    rows = normed.shape[0]
    blocks, tokens, _ = cache_hbm.shape
    heads = weight_hbm.shape[0] // (3 * HD)
    requests = length.shape[0]
    copies = fetch(
        [
            (owner_hbm, owner),
            (index_hbm, index),
            (length_hbm, length),
            (home_hbm, home),
            (moving_hbm, moving),
        ]
        + [
            (
                weight_hbm.at[3 * HD * h + HD : 3 * HD * (h + 1)],
                weight.at[PAIR * h : PAIR * (h + 1)],
            )
            for h in range(heads)
        ]
        + [(gain_hbm, gain.at[0]), (cache_hbm.at[: cache.shape[0]], cache)],
        sems,
    )
    for copy in copies[:5]:
        copy.wait()
    row = iota(owners.shape, 0)
    holders = jnp.full(owners.shape, requests, jnp.int32)
    left = jnp.zeros(owners.shape, jnp.int32)
    for b in range(blocks):
        holder = owner[0, b]
        most = jnp.where(holder < requests, length[jnp.minimum(holder, requests - 1)], 0)
        holders = jnp.where(row == b, holder, holders)
        left = jnp.where(row == b, most - index[0, b] * tokens, left)
    owners[...] = holders
    remains[...] = left
    start = lax.axis_index("kv") * rows
    replica = lax.axis_index("rep")
    at_home = row_values(home, start, rows, 128)
    target = at_home ^ row_values(moving, start, rows, 128)
    homed[...] = jnp.where(at_home == replica, 1.0, 0.0)
    serves = jnp.where(target == replica, 1.0, 0.0)
    served[...] = serves
    for copy in copies[5:-1]:
        copy.wait()
    pairs = dot_transposed(normed[...], weight[...])
    entries[...] = jnp.where(widen(serves, pairs.shape[1]) > 0.0, pairs, 0.0)
    pair = pairs.astype(BF16).astype(F32)
    keys = jnp.concatenate([pair[:, PAIR * h : PAIR * h + HD] for h in range(heads)], axis=1)
    values[...] = jnp.concatenate(
        [pair[:, PAIR * h + HD : PAIR * (h + 1)] for h in range(heads)]
        + [jnp.zeros((rows, WIDE - heads * HD), F32)],
        axis=1,
    )
    product = query[...].astype(F32)[:, : heads * HD] * keys
    head_of = iota((rows, heads * HD), 1) // HD
    own_lane = iota((rows, 128), 1) - (STATS - 256)
    self_score = jnp.full((rows, 128), VERY_LOW, F32)
    for h in range(heads):
        score = jnp.sum(jnp.where(head_of == h, product, 0.0), axis=1, keepdims=True)
        self_score = jnp.where(own_lane == h, score, self_score)
    self_scores[...] = self_score
    copies[-1].wait()


def attend_kernel(
    owner_of, remains, queries, early, cache_hbm, out, late, parts, sums, sems
):
    blocks, tokens, width = cache_hbm.shape
    ready = early.shape[0]
    copies = fetch(
        [(cache_hbm.at[b], late.at[b - ready]) for b in range(ready, blocks)], sems
    )

    def cache(b):
        return early[b] if b < ready else late[b - ready]

    heads = width // PAIR
    requests = queries.shape[0]
    rows = sums.shape[0]
    onehot = (iota((rows, requests), 1) == widen(owner_of[...], requests)).astype(BF16)
    picked = jnp.dot(onehot, queries[...], preferred_element_type=F32)
    picked = jnp.concatenate([picked, jnp.zeros((rows, width - WIDE), F32)], axis=1)
    lane = iota((rows, width), 1)
    spread = jnp.zeros((rows, width), F32)
    for h in range(heads):
        moved = picked if h == 0 else pltpu.roll(picked, HD * h, 1)
        spread = jnp.where((lane >= PAIR * h) & (lane < PAIR * h + HD), moved, spread)
    head_lane = iota((8, width), 1) - PAIR * iota((8, width), 0)
    key_lanes = (head_lane >= 0) & (head_lane < HD)
    value_lanes = (head_lane >= HD) & (head_lane < PAIR)
    block_lane = iota((8, 128), 1)
    token_lane = iota((8, tokens), 1)
    every_peak = jnp.full((8, 128), VERY_LOW, F32)
    holders = jnp.full((8, 128), requests, jnp.int32)
    scores = [None] * blocks
    uses = [None] * blocks
    peaks = [None] * blocks
    totals = [None] * blocks

    def weigh(group):
        for b in group:
            peaks[b] = jnp.max(scores[b], axis=1, keepdims=True)
        for b in group:
            weights = jnp.where(uses[b], jnp.exp(scores[b] - peaks[b]), 0.0)
            totals[b] = jnp.sum(weights, axis=1, keepdims=True)
            acc = jnp.dot(weights.astype(BF16), cache(b), preferred_element_type=F32)
            parts[b] = jnp.where(value_lanes, acc, 0.0)

    before = ()
    starts = [0] + list(range(ready, blocks, LATE_GROUP)) + [blocks]
    for g in range(len(starts) - 1):
        group = range(starts[g], starts[g + 1])
        for b in group:
            if b >= ready:
                copies[b - ready].wait()
        for b in group:
            ask = jnp.where(key_lanes, jnp.broadcast_to(spread[b : b + 1], (8, width)), 0.0)
            score = dot_transposed(ask.astype(BF16), cache(b))
            left = widen(jnp.broadcast_to(remains[b : b + 1, :], (8, 128)), tokens)
            uses[b] = token_lane < left
            scores[b] = jnp.where(uses[b], score, VERY_LOW)
        weigh(before)
        before = group
    weigh(before)
    for b in range(blocks):
        every_peak = jnp.where(block_lane == b, peaks[b], every_peak)
        holders = jnp.where(block_lane == b, owner_of[b : b + 1, :], holders)
    every_joint = every_peak
    for b in range(blocks):
        peer = jnp.where(holders == owner_of[b : b + 1, :], peaks[b], VERY_LOW)
        every_joint = jnp.maximum(every_joint, peer)
    every_factor = jnp.exp(every_peak - every_joint)
    stat_lane = iota((8, 128), 1) - (STATS - 256)
    stat_row = iota((8, 128), 0)
    stats = []
    for b in range(blocks):
        joint = every_joint[:, b : b + 1]
        factor = every_factor[:, b : b + 1]
        sums[b : b + 1, :] = jnp.sum(parts[b] * factor, axis=0, keepdims=True)
        stat = jnp.where(stat_lane == stat_row, joint, 0.0)
        stat = stat + jnp.where(stat_lane == stat_row + 8, totals[b] * factor, 0.0)
        stats.append(jnp.sum(jnp.where(stat_row < heads, stat, 0.0), axis=0, keepdims=True))
    stats += [jnp.zeros((1, 128), F32)] * (rows - blocks)
    stats = jnp.concatenate(stats, axis=0)
    sums[blocks:rows, :] = jnp.zeros((rows - blocks, width), F32)
    packed = jnp.zeros((rows, width), F32)
    every = sums[...]
    for h in range(heads):
        moved = pltpu.roll(every, width - HD * (h + 1), 1)
        packed = jnp.where((lane >= HD * h) & (lane < HD * (h + 1)), moved, packed)
    packed = packed[:, :WIDE]
    added = jnp.zeros((rows, WIDE), F32)
    added_totals = jnp.zeros((rows, 128), F32)
    first = iota((rows, 128), 0) < blocks
    for b in range(blocks):
        same = owner_of[...] == owner_of[b : b + 1, :]
        added = added + jnp.where(widen(same, WIDE), packed[b : b + 1], 0.0)
        added_totals = added_totals + jnp.where(same, stats[b : b + 1], 0.0)
        first = first & ((iota((rows, 128), 0) <= b) | ~same)
    tail = iota((rows, 128), 1) - (STATS - 256)
    peak_part = jnp.where((tail >= 0) & (tail < 8), stats, 0.0)
    total_part = jnp.where((tail >= 8) & (tail < 16), added_totals, 0.0)
    terms = jnp.zeros((rows, 128), F32)
    for k, term in enumerate(split3(peak_part + total_part)):
        terms = terms + (term if k == 0 else pltpu.roll(term, 16 * k, 1))
    last = jnp.where(tail >= 0, terms, added[:, 256:])
    full = jnp.concatenate([added[:, :256], last], axis=1)
    keep = jnp.where(first, 1.0, 0.0)
    full = jnp.where(widen(keep, WIDE) > 0.0, full, 0.0).astype(BF16)
    out[...] = lax.dot_general(
        onehot,
        full,
        (((0,), (0,)), ((), ())),
        preferred_element_type=F32,
    ).astype(BF16)


def merge_kernel(shares, self_scores, values, attended):
    rows = values.shape[0]
    count = shares.shape[0] // rows
    heads = STATS // HD
    sums = shares[...].astype(F32)
    tail = sums[:, 256:]
    joined = tail + pltpu.roll(tail, 128 - 16, 1) + pltpu.roll(tail, 128 - 32, 1)
    totals = pltpu.roll(joined, 128 - 8, 1)
    lane = iota(joined.shape, 1) - (STATS - 256)
    peaks = jnp.where((lane >= 0) & (lane < heads) & (totals > 0.0), joined, VERY_LOW)
    self_score = self_scores[...]
    top = self_score
    for s in range(count):
        top = jnp.maximum(top, peaks[s * rows : (s + 1) * rows])
    denominator = jnp.exp(self_score - top)
    self_weight = denominator.astype(BF16).astype(F32)
    wide_of = iota((rows, WIDE), 1) // HD

    def per_head(value):
        out = jnp.zeros((rows, WIDE), F32)
        for h in range(heads):
            at = STATS - 256 + h
            out = jnp.where(wide_of == h, value[:, at : at + 1], out)
        return out

    numerator = per_head(self_weight) * values[...]
    for s in range(count):
        at = slice(s * rows, (s + 1) * rows)
        factor = jnp.exp(peaks[at] - top)
        denominator = denominator + factor * totals[at]
        numerator = numerator + per_head(factor) * sums[at]
    result = numerator / jnp.where(wide_of < heads, per_head(denominator), 1.0)
    attended[...] = result.astype(BF16)


def out_kernel(homed, here, there, weight, partial):
    stay = widen(homed[...], WIDE) > 0.0
    attended = jnp.where(stay, here[...].astype(F32), there[...].astype(F32)).astype(BF16)
    partial[...] = jnp.dot(
        attended[:, : weight.shape[0]], weight[...], preferred_element_type=F32
    ).astype(BF16)


def joined(own, near, across, far):
    own, near, across, far = (v[...].astype(F32) for v in (own, near, across, far))
    return (own + near) + (across + far)


def hidden_kernel(token, own, near, far, across, gain, up, down, residual, partial):
    total = token[...].astype(F32) + joined(own, near, across, far)
    residual[...] = total
    scale = lax.rsqrt(jnp.mean(total * total, axis=-1, keepdims=True) + NORM_EPS)
    hidden = dot_transposed((total * gain[...]).astype(BF16), up[...]) * scale
    active = jax.nn.gelu(hidden, approximate=True).astype(BF16)
    partial[...] = jnp.dot(active, down[...], preferred_element_type=F32).astype(BF16)


def finish_kernel(served, residual, own, near, far, across, out):
    result = residual[...] + joined(own, near, across, far)
    out[...] = jnp.where(widen(served[...], result.shape[1]) > 0.0, result, 0.0)


def shape(dims, dtype):
    return jax.ShapeDtypeStruct(dims, dtype)


def from_others(value):
    count = lax.axis_size("tp")
    return [
        lax.ppermute(value, "tp", [(i, i ^ bits) for i in range(count)])
        for bits in (1, 3, 2)
    ]


def body(
    token_state,
    attn_gain,
    qkv_weight,
    out_weight,
    mlp_gain,
    up_weight,
    down_weight,
    kv_cache,
    home_replica,
    moving,
    cache_length,
    block_owner,
    block_index,
):
    rows, features = token_state.shape
    requests = home_replica.shape[0]
    _, blocks, tokens, width = kv_cache.shape
    heads = width // PAIR

    weight = qkv_weight.T
    spread, query, normed = pl.pallas_call(
        query_kernel,
        out_shape=(
            shape((requests, WIDE), BF16),
            shape((rows, WIDE), BF16),
            shape((rows, features), BF16),
        ),
        in_specs=[HBM] * 3,
        out_specs=(VMEM,) * 3,
        scratch_shapes=[
            pltpu.VMEM((rows, features), BF16),
            pltpu.VMEM((1, features), F32),
            pltpu.VMEM((WIDE, features), BF16),
            pltpu.SemaphoreType.DMA((2 + heads,)),
        ],
        compiler_params=PARAMS,
        name="query",
    )(*in_hbm(token_state, attn_gain, weight))
    queries = lax.all_to_all(spread, "kv", 0, 0, tiled=True)

    padded = -(-blocks // 16) * 16
    early, owners, remains, entries, homed, served, self_scores, values, gain = pl.pallas_call(
        side_kernel,
        out_shape=(
            pltpu.VMEM((EARLY, tokens, width), BF16),
            shape((padded, 128), jnp.int32),
            shape((padded, 128), jnp.int32),
            shape((rows, width), F32),
            shape((rows, 128), F32),
            shape((rows, 128), F32),
            shape((rows, 128), F32),
            shape((rows, WIDE), F32),
            shape((1, features), F32),
        ),
        in_specs=[HBM] * 8 + [VMEM] * 2,
        out_specs=(VMEM,) * 9,
        scratch_shapes=[pltpu.SMEM((1, blocks), jnp.int32)] * 2
        + [pltpu.SMEM((requests,), jnp.int32)] * 3
        + [pltpu.VMEM((width, features), BF16), pltpu.SemaphoreType.DMA((7 + heads,))],
        compiler_params=PARAMS,
        cost_estimate=pl.CostEstimate(
            flops=0, bytes_accessed=2 * EARLY * tokens * width * 2, transcendentals=0
        ),
        name="side",
    )(
        *in_hbm(
            block_owner,
            block_index,
            cache_length,
            home_replica,
            moving,
            kv_cache[0],
            weight,
            mlp_gain,
        ),
        normed,
        query,
    )

    shares = pl.pallas_call(
        attend_kernel,
        out_shape=shape((requests, WIDE), BF16),
        in_specs=[VMEM] * 4 + [HBM],
        out_specs=VMEM,
        scratch_shapes=[
            pltpu.VMEM((blocks - EARLY, tokens, width), BF16),
            pltpu.VMEM((blocks, 8, width), F32),
            pltpu.VMEM((padded, width), F32),
            pltpu.SemaphoreType.DMA((blocks - EARLY,)),
        ],
        compiler_params=PARAMS,
        name="attend",
    )(
        owners,
        remains,
        queries,
        pltpu.with_memory_space_constraint(early, pltpu.VMEM),
        *in_hbm(kv_cache[0]),
    )
    shares = lax.all_to_all(shares, "kv", 0, 0, tiled=True)

    attended = pl.pallas_call(
        merge_kernel,
        out_shape=shape((rows, WIDE), BF16),
        in_specs=[VMEM] * 3,
        out_specs=VMEM,
        compiler_params=PARAMS,
        name="merge",
    )(shares, self_scores, values)
    other = lax.ppermute(attended, "rep", [(0, 1), (1, 0)])

    partial = pl.pallas_call(
        out_kernel,
        out_shape=shape((rows, features), BF16),
        in_specs=[VMEM] * 4,
        out_specs=VMEM,
        compiler_params=PARAMS,
        name="out_projection",
    )(homed, attended, other, out_weight)

    residual, partial = pl.pallas_call(
        hidden_kernel,
        out_shape=(shape((rows, features), F32), shape((rows, features), BF16)),
        in_specs=[VMEM] * 8,
        out_specs=(VMEM,) * 2,
        compiler_params=PARAMS,
        name="hidden",
    )(token_state, partial, *from_others(partial), gain, up_weight.T, down_weight)
    result = pl.pallas_call(
        finish_kernel,
        out_shape=shape((rows, features), F32),
        in_specs=[VMEM] * 6,
        out_specs=VMEM,
        compiler_params=PARAMS,
        name="finish",
    )(served, residual, partial, *from_others(partial))
    return (result[None], entries[None])


def solution(mesh):
    return jax.shard_map(
        body,
        mesh=mesh,
        in_specs=(
            P("kv", None),
            P(),
            P(None, "tp"),
            P("tp", None),
            P(),
            P(None, "tp"),
            P("tp", None),
            P("rep", "kv", None, "tp"),
            P(),
            P(),
            P(),
            P("rep", "kv"),
            P("rep", "kv"),
        ),
        out_specs=(P("rep", "kv", None), P("rep", "kv", "tp")),
        check_vma=False,
    )
```
